32 devices in a mesh: member: 4 (over y, x), slab: 8 (over z, core).
Axes of the slice: x: 2, y: 2, z: 4, core: 2. Of those that a mesh axis runs over, the one named last changes fastest.
Arguments:
- control: float32 [16, 2, 1024, 2048], P('member', None, 'slab'), may hold values from -6 to 6
- perturbation: bfloat16 [16, 2, 1024, 2048], P('member', None, 'slab'), may hold values from -6 to 6
- loc_row: float32 [2, 1024], P(None, 'slab'), may hold values from 0.2 to 2
- loc_col: float32 [2, 2048], replicated, may hold values from 0.2 to 2
- obs_tile: int32 [2048], P('slab'), may hold values from 0 to 4095, as said below
- obs_count: int32 [2048], P('slab'), may hold values from 1 to 128
- obs_value: float32 [2048, 128], P('slab'), may hold values from -12 to 12
Outputs:
- gradient: float32 [16, 2, 1024, 2048], P('member', None, 'slab')
The draws below stay inside these ranges and needn't reach their ends.
Inputs may be any that keep to these rules, and one draw needn't show every extreme that they name: `obs_tile`: entry i names a tile of slab block i // 256 in that block's numbering, whose columns lie in column share k = (i mod 256) // (256 / 8), i.e. columns k * 2048 / 8 onward; tiles may repeat. cells 0 to obs_count - 1 of a tile are observed.
All inputs are finite; a program needn't handle non-finite values.
Results may differ from the reference program's by a relative error of at most 0.012.
Values may be sent and summed in bfloat16 or wider, within the bound.
A program may use at most 64 MiB of HBM per device.

```python
import math
import jax
import jax.numpy as jnp
from jax import lax

NY = 1024
NX = 2048
LEV = 2
TILE = 128
OBS_DEV = 256
MEMBERS = 16
OBS = 2048
TILES_DEV = 4096
N_SLAB = 8


def draw_obs_tile(key, part):
    rows = NY // N_SLAB
    per_row = NX // TILE
    per_share = NX // N_SLAB // TILE
    index = jnp.arange(OBS, dtype=jnp.int32)
    share = index % OBS_DEV // (OBS_DEV // N_SLAB)
    key_level = jax.random.fold_in(key, 11)
    key_row = jax.random.fold_in(key, 23)
    key_within = jax.random.fold_in(key, 37)
    level = jax.random.randint(key_level, (OBS,), 0, LEV, dtype=jnp.int32)
    row_in = jax.random.randint(key_row, (OBS,), 0, rows, dtype=jnp.int32)
    within = jax.random.randint(key_within, (OBS,), 0, per_share, dtype=jnp.int32)
    column_tile = share * per_share + within
    return ((level * rows + row_in) * per_row + column_tile).astype(jnp.int32)


def touch_ends(values, stream_key, smallest, top_value):
    place = [jax.random.randint(jax.random.fold_in(stream_key, axis), (), 0, length) for axis, length in enumerate(values.shape)]
    longest = values.shape.index(max(values.shape))
    next_to = place[:longest] + [(place[longest] + 1) % values.shape[longest]] + place[longest + 1:]
    return values.at[tuple(place)].set(smallest).at[tuple(next_to)].set(top_value)


def block_levels(rng, extent, split, low, top_value):
    gain = 1.0
    for dim, blocks in split:
        heights = jax.random.uniform(jax.random.fold_in(jax.random.fold_in(rng, 6), dim), (blocks,), jnp.float32, low / len(split), top_value / len(split))
        gain = gain * jnp.repeat(jnp.exp(heights), extent[dim] // blocks).reshape((-1,) + (1,) * (len(extent) - 1 - dim))
    return gain


def scatter_about(own_key, extent, scale, bound, split=(), kind=jnp.bfloat16):
    array = scale * jax.random.normal(own_key, extent, jnp.float32)
    if split:
        array = array * block_levels(own_key, extent, split, -0.22, 0.18)
    return jnp.clip(array, -bound, bound).astype(kind)


def setup_inputs(seed: int = 0) -> dict:
    seeds = jax.random.split(jax.random.key(seed), 8)
    control = scatter_about(seeds[0], (MEMBERS, LEV, NY, NX), 1.0, 6.0, ((0, 4), (2, 8)), jnp.float32)
    perturbation = scatter_about(seeds[1], (MEMBERS, LEV, NY, NX), 1.0, 6.0, ((0, 4), (2, 8)))
    loc_row = jnp.clip(jnp.exp(math.log(2.0) - 2.3025851 * jax.random.uniform(seeds[2], (LEV, NY), jnp.float32) ** block_levels(seeds[2], (LEV, NY), ((1, 8),), -0.2, 0.2)), 0.2, 2.0)
    loc_col = jnp.clip(jnp.exp(jax.random.uniform(seeds[3], (LEV, NX), jnp.float32, math.log(0.2), math.log(2.0))), 0.2, 2.0)
    obs_tile = draw_obs_tile(jax.random.fold_in(seeds[7], 71), 0)
    obs_count = touch_ends(jax.random.randint(seeds[5], (OBS,), 1, TILE + 1), jax.random.fold_in(seeds[5], 1), 1, TILE).astype(jnp.int32)
    obs_value = scatter_about(seeds[6], (OBS, TILE), 2.0, 12.0, ((0, 8),), jnp.float32)
    return dict(control=control, perturbation=perturbation, loc_row=loc_row, loc_col=loc_col, obs_tile=obs_tile, obs_count=obs_count, obs_value=obs_value)


def hartley(order):
    index = jnp.arange(order, dtype=jnp.int32)
    product = index[:, None] * index[None, :] % order
    angle = 2.0 * jnp.pi * product.astype(jnp.float32) / order
    table = (jnp.cos(angle) + jnp.sin(angle)) / jnp.sqrt(jnp.float32(order))
    return table.astype(jnp.bfloat16).astype(jnp.float32)

def rounded(value):
    return lax.optimization_barrier(value.astype(jnp.bfloat16)).astype(jnp.float32)

def reference(control, perturbation, loc_row, loc_col, obs_tile, obs_count, obs_value):
    table_y = hartley(NY)
    table_x = hartley(NX)
    amplitude = loc_row[:, :, None] * loc_col[:, None, :]

    def forward(carry, pair):
        coeffs, member_pert = pair
        scaled = rounded(coeffs * amplitude)
        along = rounded(jnp.einsum('lab,bx->lax', scaled, table_x))
        field = rounded(jnp.einsum('ya,lax->lyx', table_y, along))
        return (carry + member_pert.astype(jnp.float32) * field, None)
    start = jnp.zeros((LEV, NY, NX), jnp.float32)
    increment, _ = lax.scan(forward, start, (control, perturbation))
    rows = NY // N_SLAB
    tiled = increment.reshape(LEV, N_SLAB, rows, NX // TILE, TILE)
    tiled = jnp.transpose(tiled, (1, 0, 2, 3, 4)).reshape(N_SLAB, TILES_DEV, TILE)
    block = (jnp.arange(OBS, dtype=jnp.int32) // OBS_DEV).astype(jnp.int32)
    cells = tiled[block, obs_tile]
    resid = cells - obs_value
    observed = jnp.arange(TILE, dtype=jnp.int32)[None, :] < obs_count[:, None]
    score = jnp.where(observed, resid / jnp.sqrt(1.0 + resid * resid / 4.0), 0.0)
    spread = jnp.zeros((N_SLAB, TILES_DEV, TILE), jnp.float32).at[block, obs_tile].add(score)
    spread = spread.reshape(N_SLAB, LEV, rows, NX // TILE, TILE)
    adjoint_field = jnp.transpose(spread, (1, 0, 2, 3, 4)).reshape(LEV, NY, NX)

    def adjoint(member_pert):
        weighted = rounded(member_pert.astype(jnp.float32) * adjoint_field)
        back = rounded(jnp.einsum('ay,lyx->lax', table_y, weighted))
        return amplitude * jnp.einsum('lax,xb->lab', back, table_x)
    return lax.map(adjoint, perturbation)
```

```python
import functools
import math

import jax
import jax.numpy as jnp
from jax import lax
from jax.experimental import pallas as pl
from jax.experimental.pallas import tpu as pltpu
from jax.sharding import PartitionSpec as P

TILE = 128
HALF = TILE // 2
BF = jnp.bfloat16
F32 = jnp.float32
MESH = pl.DeviceIdType.MESH
VM = pl.BlockSpec(memory_space=pltpu.VMEM)


def turn(product, order):
    angle = (2.0 * math.pi / order) * (product % order).astype(F32)
    return jnp.cos(angle), jnp.sin(angle)


def column_table(column, order, depth):
    step = 32
    outer = jnp.arange(depth // step, dtype=jnp.int32)[:, None] * step
    inner = jnp.arange(step, dtype=jnp.int32)[:, None]
    ca, sa = turn(outer * column[None, :], order)
    cb, sb = turn(inner * column[None, :], order)
    scale = 1.0 / math.sqrt(order)
    plus, minus = (cb + sb) * scale, (cb - sb) * scale
    table = ca[:, None, :] * plus[None] + sa[:, None, :] * minus[None]
    return table.astype(BF).reshape(depth, column.shape[0])


def low_half(shape):
    return lax.broadcasted_iota(jnp.int32, shape, 1) < HALF


def cell_of_lane(lane, parity):
    high = (lane >= HALF).astype(jnp.int32)
    return 2 * (lane - HALF * high) + jnp.where(parity == 0, high, 1 - high)


def pick_kernel(rows, per_row, tile_ref, count_ref, value_ref, pert_ref, pert_out, value_out, seen_out):
    members, levels = pert_ref.shape[:2]
    n = tile_ref.shape[1]
    tile = tile_ref[0]
    level_row = tile // per_row
    parity = tile % 2
    hot = (lax.broadcasted_iota(jnp.int32, (n, levels * rows), 1) == level_row).astype(BF)
    lane = lax.broadcasted_iota(jnp.int32, (TILE, TILE), 1)
    cell = lax.broadcasted_iota(jnp.int32, (TILE, TILE), 0)
    move0 = (cell == cell_of_lane(lane, 0)).astype(F32)
    move1 = (cell == cell_of_lane(lane, 1)).astype(F32)
    for m in range(members):
        block = pert_ref[m].reshape(levels * rows, 2 * TILE)
        both = jnp.dot(hot, block, preferred_element_type=F32).astype(BF)
        first = jnp.dot(both[:, :TILE], move0.astype(BF), preferred_element_type=F32)
        second = jnp.dot(both[:, TILE:], move1.astype(BF), preferred_element_type=F32)
        pert_out[m * n : (m + 1) * n, :] = jnp.where(parity == 0, first, second).astype(BF)
    value = value_ref[0]
    first = jnp.dot(value, move0, precision=lax.Precision.HIGHEST, preferred_element_type=F32)
    second = jnp.dot(value, move1, precision=lax.Precision.HIGHEST, preferred_element_type=F32)
    value_out[0] = jnp.where(parity == 0, first, second)
    cells = cell_of_lane(lax.broadcasted_iota(jnp.int32, (n, TILE), 1), parity)
    seen_out[0] = (cells < count_ref[0]).astype(F32)


def along_kernel(control_ref, row_ref, col_ref, even_ref, odd_ref, ev_ref, od_ref):
    levels, rows, width = control_ref.shape[1:]
    half = width // 2
    plus, minus = [], []
    for l in range(levels):
        row = row_ref[l]
        a = control_ref[0, l, :, :half] * (row * col_ref[l : l + 1, :half])
        b = control_ref[0, l, :, half:] * (row * col_ref[l : l + 1, half:])
        plus.append((a + b).astype(BF))
        minus.append((a - b).astype(BF))
    plus = jnp.concatenate(plus, 0)
    minus = jnp.concatenate(minus, 0)
    ev_ref[...] = jnp.dot(plus, even_ref[...], preferred_element_type=F32).astype(BF)
    od_ref[...] = jnp.dot(minus, odd_ref[...], preferred_element_type=F32).astype(BF)


def by_level(table, level, levels):
    return jnp.concatenate([jnp.where(level == l, table, jnp.zeros_like(table)) for l in range(levels)], 1)


def forward_kernel(members, levels, h_ref, level_ref, parity_ref, ev_ref, od_ref, *rest):
    pieces, out_ref = rest[:-1], rest[-1]
    total = h_ref.shape[1]
    each = total // len(pieces)
    depth = ev_ref.shape[0] // members
    hm = by_level(h_ref[0], level_ref[0], levels)
    straight = low_half((total, TILE)) == (parity_ref[0] == 0)
    acc = jnp.zeros((total, TILE), F32)
    for m in range(members):
        f = jnp.dot(hm, ev_ref[m * depth : (m + 1) * depth, :], preferred_element_type=F32)
        g = jnp.dot(hm, od_ref[m * depth : (m + 1) * depth, :], preferred_element_type=F32)
        pert = jnp.concatenate([p[m * each : (m + 1) * each, :] for p in pieces], 0).astype(F32)
        acc += pert * jnp.where(straight, f, g)
    out_ref[0] = acc.astype(BF)


def backward_kernel(members, levels, h_ref, level_ref, parity_ref, score_ref, *rest):
    pieces, (ev_ref, od_ref) = rest[:-2], rest[-2:]
    total = h_ref.shape[1]
    each = total // len(pieces)
    hm = by_level(h_ref[0], level_ref[0], levels)
    straight = low_half((total, TILE)) == (parity_ref[0] == 0)
    score = score_ref[...].reshape(total, TILE).astype(F32)
    depth = hm.shape[1]
    over = (((0,), (0,)), ((), ()))
    for m in range(members):
        pert = jnp.concatenate([p[m * each : (m + 1) * each, :] for p in pieces], 0).astype(F32)
        w = pert * score
        we = jnp.where(straight, w, 0.0).astype(BF)
        wo = jnp.where(straight, 0.0, w).astype(BF)
        both = lax.dot_general(hm, jnp.concatenate([we, wo], 1), over, preferred_element_type=F32)
        ev_ref[m * depth : (m + 1) * depth, :] = both[:, :TILE].astype(BF)
        od_ref[m * depth : (m + 1) * depth, :] = both[:, TILE:].astype(BF)


def gradient_kernel(ev_ref, od_ref, row_ref, col_ref, even_ref, odd_ref, out_ref):
    levels, rows, width = out_ref.shape[1:]
    half = width // 2
    over = (((1,), (1,)), ((), ()))
    chunk = 512
    for c in range(0, half, chunk):
        e = lax.dot_general(ev_ref[...], even_ref[c : c + chunk, :], over, preferred_element_type=F32)
        o = lax.dot_general(od_ref[...], odd_ref[c : c + chunk, :], over, preferred_element_type=F32)
        for l in range(levels):
            el, ol = e[l * rows : (l + 1) * rows], o[l * rows : (l + 1) * rows]
            row = row_ref[l]
            out_ref[0, l, :, c : c + chunk] = (el + ol) * (row * col_ref[l : l + 1, c : c + chunk])
            out_ref[0, l, :, half + c : half + c + chunk] = (el - ol) * (
                row * col_ref[l : l + 1, half + c : half + c + chunk]
            )


def exchange_kernel(groups, slabs, part_ref, value_ref, seen_ref, out_ref,
                    land_a, pack_b, land_b, mine_c, land_c, send, recv):
    r = lax.axis_index("member")
    s = lax.axis_index("slab")
    chunk = part_ref.shape[0] // groups
    barrier = pltpu.get_barrier_semaphore()
    for d in range(1, groups):
        pl.semaphore_signal(barrier, inc=1, device_id=(lax.rem(r + d, groups), s), device_id_type=MESH)
    for d in range(1, slabs):
        pl.semaphore_signal(barrier, inc=1, device_id=(r, lax.rem(s + d, slabs)), device_id_type=MESH)
    pl.semaphore_wait(barrier, groups + slabs - 2)

    def copy(src, dst, k, where):
        c = pltpu.make_async_remote_copy(
            src_ref=src, dst_ref=dst, send_sem=send.at[k], recv_sem=recv.at[k],
            device_id=where, device_id_type=MESH,
        )
        c.start()
        return c

    k = 0
    copies = []
    for d in range(1, groups):
        to = lax.rem(r + d, groups)
        copies.append(copy(part_ref.at[pl.ds(to * chunk, chunk)], land_a.at[d - 1], k, (to, s)))
        k += 1
    total = part_ref[pl.ds(r * chunk, chunk)].astype(F32)
    for d, c in enumerate(copies):
        c.wait()
        total += land_a[d].astype(F32)
    for j in range(slabs):
        pack_b[j] = total[:, j].astype(BF)
    copies = []
    for d in range(1, slabs):
        copies.append(copy(pack_b.at[d], land_b.at[d - 1], k, (r, lax.rem(s + slabs - d, slabs))))
        k += 1
    cells = total[:, 0]
    for d, c in enumerate(copies):
        c.wait()
        cells += land_b[d].astype(F32)
    resid = cells - value_ref[pl.ds(r * chunk, chunk)]
    score = resid / jnp.sqrt(1.0 + resid * resid / 4.0)
    score = jnp.where(seen_ref[pl.ds(r * chunk, chunk)] > 0.5, score, 0.0).astype(BF)
    mine_c[...] = score
    land_c[0] = score
    copies = []
    for d in range(1, slabs):
        copies.append(copy(mine_c, land_c.at[d], k, (r, lax.rem(s + d, slabs))))
        k += 1
    for c in copies:
        c.wait()
    copies = []
    for d in range(1, groups):
        copies.append(copy(land_c, out_ref.at[r], k, (lax.rem(r + d, groups), s)))
        k += 1
    out_ref[r] = land_c[...]
    for c in copies:
        c.wait()


def shards(control, perturbation, loc_row, loc_col, obs_tile, obs_count, obs_value):
    members, levels, rows, width = control.shape
    slabs = lax.axis_size("slab")
    groups = lax.axis_size("member")
    height = rows * slabs
    half = width // 2
    blocks = width // (2 * TILE)
    n_obs = obs_tile.shape[0]
    each = n_obs // blocks
    total = slabs * each
    depth = levels * rows
    chunk = blocks // groups
    per_row = width // TILE
    mine = lax.axis_index("slab")
    assert slabs % blocks == 0 and blocks % groups == 0

    stack = members * each
    picked, value, seen = pl.pallas_call(
        functools.partial(pick_kernel, rows, per_row),
        grid=(blocks,),
        in_specs=[
            pl.BlockSpec((1, each, 1), lambda q: (q, 0, 0)),
            pl.BlockSpec((1, each, 1), lambda q: (q, 0, 0)),
            pl.BlockSpec((1, each, TILE), lambda q: (q, 0, 0)),
            pl.BlockSpec((members, levels, rows, 2 * TILE), lambda q: (0, 0, 0, q)),
        ],
        out_specs=[
            pl.BlockSpec((stack, TILE), lambda q: (q, 0)),
            pl.BlockSpec((1, each, TILE), lambda q: (q, 0, 0)),
            pl.BlockSpec((1, each, TILE), lambda q: (q, 0, 0)),
        ],
        out_shape=[
            jax.ShapeDtypeStruct((blocks * stack, TILE), BF),
            jax.ShapeDtypeStruct((blocks, each, TILE), F32),
            jax.ShapeDtypeStruct((blocks, each, TILE), F32),
        ],
        name="pick",
    )(
        obs_tile.reshape(blocks, each, 1),
        obs_count.reshape(blocks, each, 1),
        obs_value.reshape(blocks, each, TILE),
        perturbation,
    )
    level = obs_tile // (rows * per_row)
    row_in = obs_tile // per_row % rows
    code = level * 2 + obs_tile % 2
    meta = jnp.concatenate([row_in, code]).astype(BF).reshape(-1, TILE)
    meta = jnp.pad(meta, ((0, -meta.shape[0] % 16), (0, 0)))
    payload = jnp.concatenate([picked, meta], 0)
    pieces = [payload]
    for d in range(1, slabs):
        ring = [(i, (i + d) % slabs) for i in range(slabs)]
        pieces.append(lax.ppermute(payload, "slab", ring))

    column = jnp.arange(half, dtype=jnp.int32)
    swapped = column - column % TILE + (column % TILE + HALF) % TILE
    table_even = column_table(2 * column, width, half)
    table_odd = column_table(2 * swapped + 1, width, half)

    row_col = loc_row[:, :, None]
    table_spec = pl.BlockSpec((half, half), lambda m: (0, 0))
    row_spec = pl.BlockSpec((levels, rows, 1), lambda m: (0, 0, 0))
    col_spec = pl.BlockSpec((levels, width), lambda m: (0, 0))
    big_spec = pl.BlockSpec((1, levels, rows, width), lambda m: (m, 0, 0, 0))
    half_spec = pl.BlockSpec((depth, half), lambda m: (m, 0))
    half_shape = jax.ShapeDtypeStruct((members * depth, half), BF)
    flops = 4 * members * depth * half * half
    along_ev, along_od = pl.pallas_call(
        along_kernel,
        grid=(members,),
        in_specs=[big_spec, row_spec, col_spec, table_spec, table_spec],
        out_specs=[half_spec, half_spec],
        out_shape=[half_shape, half_shape],
        cost_estimate=pl.CostEstimate(flops=flops, bytes_accessed=16 << 20, transcendentals=0),
        name="along",
    )(control, row_col, loc_col, table_even, table_odd)

    first = blocks * stack
    k = n_obs // TILE
    rows_of = jnp.stack([p[first : first + k].reshape(blocks, each) for p in pieces], 1)
    code_of = jnp.stack([p[first + k : first + 2 * k].reshape(blocks, each) for p in pieces], 1)
    source = (mine - jnp.arange(slabs, dtype=jnp.int32)) % slabs
    y = source[None, :, None] * rows + rows_of.astype(jnp.int32)
    y = y.reshape(blocks, total, 1)
    code_of = code_of.astype(jnp.int32).reshape(blocks, total, 1)
    level_of, parity_of = code_of // 2, code_of % 2
    a = mine * rows + jnp.arange(rows, dtype=jnp.int32)
    ch, sh = turn(y * a, height)
    table_h = ((ch + sh) * (1.0 / math.sqrt(height))).astype(BF)

    h_spec = pl.BlockSpec((1, total, rows), lambda q: (q, 0, 0))
    one_spec = pl.BlockSpec((1, total, 1), lambda q: (q, 0, 0))
    piece_spec = pl.BlockSpec((stack, TILE), lambda q: (q, 0))
    strip_spec = pl.BlockSpec((members * depth, TILE), lambda q: (0, q))
    part = pl.pallas_call(
        functools.partial(forward_kernel, members, levels),
        grid=(blocks,),
        in_specs=[h_spec, one_spec, one_spec, strip_spec, strip_spec] + [piece_spec] * slabs,
        out_specs=pl.BlockSpec((1, total, TILE), lambda q: (q, 0, 0)),
        out_shape=jax.ShapeDtypeStruct((blocks, total, TILE), BF),
        name="forward",
    )(table_h, level_of, parity_of, along_ev, along_od, *pieces)

    n_copies = 2 * (groups + slabs - 2)
    score = pl.pallas_call(
        functools.partial(exchange_kernel, groups, slabs),
        in_specs=[VM, VM, VM],
        out_specs=VM,
        out_shape=jax.ShapeDtypeStruct((groups, slabs, chunk, each, TILE), BF),
        scratch_shapes=[
            pltpu.VMEM((groups - 1, chunk, slabs, each, TILE), BF),
            pltpu.VMEM((slabs, chunk, each, TILE), BF),
            pltpu.VMEM((slabs - 1, chunk, each, TILE), BF),
            pltpu.VMEM((chunk, each, TILE), BF),
            pltpu.VMEM((slabs, chunk, each, TILE), BF),
            pltpu.SemaphoreType.DMA((n_copies,)),
            pltpu.SemaphoreType.DMA((n_copies,)),
        ],
        compiler_params=pltpu.CompilerParams(collective_id=0, has_side_effects=True),
        name="exchange",
    )(part.reshape(blocks, slabs, each, TILE), value, seen)

    back_ev, back_od = pl.pallas_call(
        functools.partial(backward_kernel, members, levels),
        grid=(blocks,),
        in_specs=[
            h_spec, one_spec, one_spec,
            pl.BlockSpec((1, slabs, 1, each, TILE), lambda q: (q // chunk, 0, q % chunk, 0, 0)),
        ] + [piece_spec] * slabs,
        out_specs=[strip_spec, strip_spec],
        out_shape=[half_shape, half_shape],
        name="backward",
    )(table_h, level_of, parity_of, score, *pieces)

    return pl.pallas_call(
        gradient_kernel,
        grid=(members,),
        in_specs=[half_spec, half_spec, row_spec, col_spec, table_spec, table_spec],
        out_specs=big_spec,
        out_shape=jax.ShapeDtypeStruct(control.shape, F32),
        cost_estimate=pl.CostEstimate(flops=flops, bytes_accessed=16 << 20, transcendentals=0),
        name="gradient",
    )(back_ev, back_od, row_col, loc_col, table_even, table_odd)


def solution(mesh):
    placed = (
        P("member", None, "slab", None),
        P("member", None, "slab", None),
        P(None, "slab"),
        P(),
        P("slab"),
        P("slab"),
        P("slab", None),
    )
    return jax.shard_map(
        shards,
        mesh=mesh,
        in_specs=placed,
        out_specs=P("member", None, "slab", None),
        check_vma=False,
    )
```

```python
import functools
import math

import jax
import jax.numpy as jnp
from jax import lax
from jax.experimental import pallas as pl
from jax.experimental.pallas import tpu as pltpu
from jax.sharding import PartitionSpec as P

TILE = 128
HALF = TILE // 2
BF = jnp.bfloat16
F32 = jnp.float32
MESH = pl.DeviceIdType.MESH
VM = pl.BlockSpec(memory_space=pltpu.VMEM)


def turn(product, order):
    angle = (2.0 * math.pi / order) * (product % order).astype(F32)
    return jnp.cos(angle), jnp.sin(angle)


def column_table(column, order, depth):
    step = 32
    outer = jnp.arange(depth // step, dtype=jnp.int32)[:, None] * step
    inner = jnp.arange(step, dtype=jnp.int32)[:, None]
    ca, sa = turn(outer * column[None, :], order)
    cb, sb = turn(inner * column[None, :], order)
    scale = 1.0 / math.sqrt(order)
    plus, minus = (cb + sb) * scale, (cb - sb) * scale
    table = ca[:, None, :] * plus[None] + sa[:, None, :] * minus[None]
    return table.astype(BF).reshape(depth, column.shape[0])


def low_half(shape):
    return lax.broadcasted_iota(jnp.int32, shape, 1) < HALF


def cell_of_lane(lane, parity):
    high = (lane >= HALF).astype(jnp.int32)
    return 2 * (lane - HALF * high) + jnp.where(parity == 0, high, 1 - high)


def pick_kernel(rows, per_row, tile_ref, count_ref, value_ref, pert_ref, pert_out, value_out, seen_out):
    members, levels = pert_ref.shape[:2]
    n = tile_ref.shape[1]
    tile = tile_ref[0]
    level_row = tile // per_row
    parity = tile % 2
    hot = (lax.broadcasted_iota(jnp.int32, (n, levels * rows), 1) == level_row).astype(BF)
    lane = lax.broadcasted_iota(jnp.int32, (TILE, TILE), 1)
    cell = lax.broadcasted_iota(jnp.int32, (TILE, TILE), 0)
    move0 = (cell == cell_of_lane(lane, 0)).astype(F32)
    move1 = (cell == cell_of_lane(lane, 1)).astype(F32)
    for m in range(members):
        block = pert_ref[m].reshape(levels * rows, 2 * TILE)
        both = jnp.dot(hot, block, preferred_element_type=F32).astype(BF)
        first = jnp.dot(both[:, :TILE], move0.astype(BF), preferred_element_type=F32)
        second = jnp.dot(both[:, TILE:], move1.astype(BF), preferred_element_type=F32)
        pert_out[m * n : (m + 1) * n, :] = jnp.where(parity == 0, first, second).astype(BF)
    value = value_ref[0]
    first = jnp.dot(value, move0, precision=lax.Precision.HIGHEST, preferred_element_type=F32)
    second = jnp.dot(value, move1, precision=lax.Precision.HIGHEST, preferred_element_type=F32)
    value_out[0] = jnp.where(parity == 0, first, second)
    cells = cell_of_lane(lax.broadcasted_iota(jnp.int32, (n, TILE), 1), parity)
    seen_out[0] = (cells < count_ref[0]).astype(F32)


def along_kernel(control_ref, row_ref, col_ref, even_ref, odd_ref, out_ref):
    levels, rows, width = control_ref.shape[1:]
    half = width // 2
    plus, minus = [], []
    for l in range(levels):
        row = row_ref[l]
        a = control_ref[0, l, :, :half] * (row * col_ref[l : l + 1, :half])
        b = control_ref[0, l, :, half:] * (row * col_ref[l : l + 1, half:])
        plus.append((a + b).astype(BF))
        minus.append((a - b).astype(BF))
    plus = jnp.concatenate(plus, 0)
    minus = jnp.concatenate(minus, 0)
    even = jnp.dot(plus, even_ref[...], preferred_element_type=F32).astype(BF)
    odd = jnp.dot(minus, odd_ref[...], preferred_element_type=F32).astype(BF)
    for q in range(out_ref.shape[0]):
        out_ref[q, :, :TILE] = even[:, q * TILE : (q + 1) * TILE]
        out_ref[q, :, TILE:] = odd[:, q * TILE : (q + 1) * TILE]


def by_level(table, level, levels):
    return jnp.concatenate([jnp.where(level == l, table, jnp.zeros_like(table)) for l in range(levels)], 1)


def other_core(index, e):
    return index + e * (1 - 2 * lax.rem(index, 2))


def tiles_kernel(slabs, tile_ref, out_ref, send, recv):
    r = lax.axis_index("member")
    s = lax.axis_index("slab")
    barrier = pltpu.get_barrier_semaphore()
    for d in range(1, slabs):
        pl.semaphore_signal(barrier, inc=1, device_id=(r, lax.rem(s + d, slabs)), device_id_type=MESH)
    pl.semaphore_wait(barrier, slabs - 1)
    copies = []
    for k in range(1, slabs):
        e, i = k % 2, k // 2
        c = pltpu.make_async_remote_copy(
            src_ref=tile_ref, dst_ref=out_ref.at[e, i], send_sem=send.at[k], recv_sem=recv.at[k],
            device_id=(r, other_core(lax.rem(s + 2 * i, slabs), e)), device_id_type=MESH,
        )
        c.start()
        copies.append(c)
    out_ref[0, 0] = tile_ref[...]
    for c in copies:
        c.wait()


def core_kernel(members, levels, groups, slabs, h_ref, code_ref, along_ref, value_ref, seen_ref, *rest):
    pairs = slabs // 2
    pieces, rest = rest[:pairs], rest[pairs:]
    back_ref, swapped, part, land_a, pack_b, land_b, mine_c, land_c, land_d, send, recv = rest
    r = lax.axis_index("member")
    s = lax.axis_index("slab")
    blocks, _, n, _ = h_ref.shape
    chunk = blocks // groups
    depth = along_ref.shape[1] // members
    each = n // pairs
    stack = members * each
    barrier = pltpu.get_barrier_semaphore()
    for d in range(1, groups):
        pl.semaphore_signal(barrier, inc=1, device_id=(lax.rem(r + d, groups), s), device_id_type=MESH)
    for d in range(1, slabs):
        pl.semaphore_signal(barrier, inc=1, device_id=(r, lax.rem(s + d, slabs)), device_id_type=MESH)
    pl.semaphore_wait(barrier, groups + slabs - 2)
    used = [0]

    def copy(src, dst, where):
        k = used[0]
        used[0] += 1
        c = pltpu.make_async_remote_copy(
            src_ref=src, dst_ref=dst, send_sem=send.at[k], recv_sem=recv.at[k],
            device_id=where, device_id_type=MESH,
        )
        c.start()
        return c

    swaps = [copy(pieces[i], swapped.at[i], (r, other_core(s, 1))) for i in range(pairs)]

    def pert_rows(q, e, m):
        at = pl.ds(pl.multiple_of(q * stack + m * each, each), each)
        rows = [swapped[i, at, :] if e else pieces[i][at, :] for i in range(pairs)]
        return jnp.concatenate(rows, 0).astype(F32)

    def forward(q, e):
        code = code_ref[q, e]
        hm = by_level(h_ref[q, e], code // 2, levels)
        straight = low_half((n, TILE)) == (code % 2 == 0)
        acc = jnp.zeros((n, TILE), F32)
        for m in range(members):
            fg = jnp.dot(hm, along_ref[q, m * depth : (m + 1) * depth, :], preferred_element_type=F32)
            acc += pert_rows(q, e, m) * jnp.where(straight, fg[:, :TILE], fg[:, TILE:])
        part[q, e] = acc.astype(BF).reshape(pairs, each, TILE)

    @pl.loop(0, blocks)
    def _(q):
        forward(q, 0)

    for c in swaps:
        c.wait()
    copies = []
    for d in list(range(1, groups)) + [0]:
        to = lax.rem(r + d, groups)

        @pl.loop(0, chunk)
        def _(u):
            forward(to * chunk + u, 1)

        if d:
            copies.append(copy(part.at[pl.ds(to * chunk, chunk)], land_a.at[d - 1], (to, s)))

    total = part[pl.ds(r * chunk, chunk)].astype(F32)
    for d, c in enumerate(copies):
        c.wait()
        total += land_a[d].astype(F32)
    for e in range(2):
        for i in range(pairs):
            pack_b[e, i] = total[:, e, i].astype(BF)
    cells = total[:, 0, 0]
    copies = []
    for k in range(1, slabs):
        e, i = k % 2, k // 2
        to = other_core(lax.rem(s + slabs - 2 * i, slabs), e)
        copies.append(copy(pack_b.at[e, i], land_b.at[k - 1], (r, to)))
    for k, c in enumerate(copies):
        c.wait()
        cells += land_b[k].astype(F32)
    resid = cells - value_ref[pl.ds(r * chunk, chunk)]
    score = resid / jnp.sqrt(1.0 + resid * resid / 4.0)
    score = jnp.where(seen_ref[pl.ds(r * chunk, chunk)] > 0.5, score, 0.0).astype(BF)
    mine_c[...] = score
    land_c[0, 0] = score
    copies = []
    for k in range(1, slabs):
        e, i = k % 2, k // 2
        to = other_core(lax.rem(s + 2 * i, slabs), e)
        copies.append(copy(mine_c, land_c.at[e, i], (r, to)))
    for c in copies:
        c.wait()
    copies = []
    for d in range(1, groups):
        copies.append(copy(land_c, land_d.at[d - 1], (lax.rem(r + d, groups), s)))
    over = (((0,), (0,)), ((), ()))

    def backward(q, read):
        hm = jnp.concatenate([by_level(h_ref[q, e], code_ref[q, e] // 2, levels) for e in range(2)], 0)
        code = jnp.concatenate([code_ref[q, 0], code_ref[q, 1]], 0)
        straight = low_half((2 * n, TILE)) == (code % 2 == 0)
        score = jnp.concatenate([read(e, i) for e in range(2) for i in range(pairs)], 0).astype(F32)
        for m in range(members):
            w = jnp.concatenate([pert_rows(q, 0, m), pert_rows(q, 1, m)], 0) * score
            both = jnp.concatenate([jnp.where(straight, w, 0.0), jnp.where(straight, 0.0, w)], 1)
            out = lax.dot_general(hm, both.astype(BF), over, preferred_element_type=F32)
            back_ref[q, m * depth : (m + 1) * depth, :] = out.astype(BF)

    @pl.loop(0, chunk)
    def _(u):
        backward(r * chunk + u, lambda e, i: land_c[e, i, u])

    for d in range(1, groups):
        copies[groups - 1 - d].wait()
        source = lax.rem(r + d, groups)

        @pl.loop(0, chunk)
        def _(u):
            backward(source * chunk + u, lambda e, i: land_d[groups - 1 - d, e, i, u])


def gradient_kernel(back_ref, row_ref, col_ref, even_ref, odd_ref, out_ref):
    levels, rows, width = out_ref.shape[1:]
    half = width // 2
    over = (((1,), (1,)), ((), ()))
    chunk = 512
    blocks = back_ref.shape[0]
    ev = jnp.concatenate([back_ref[q, :, :TILE] for q in range(blocks)], 1)
    od = jnp.concatenate([back_ref[q, :, TILE:] for q in range(blocks)], 1)
    for c in range(0, half, chunk):
        e = lax.dot_general(ev, even_ref[c : c + chunk, :], over, preferred_element_type=F32)
        o = lax.dot_general(od, odd_ref[c : c + chunk, :], over, preferred_element_type=F32)
        for l in range(levels):
            el, ol = e[l * rows : (l + 1) * rows], o[l * rows : (l + 1) * rows]
            row = row_ref[l]
            out_ref[0, l, :, c : c + chunk] = (el + ol) * (row * col_ref[l : l + 1, c : c + chunk])
            out_ref[0, l, :, half + c : half + c + chunk] = (el - ol) * (
                row * col_ref[l : l + 1, half + c : half + c + chunk]
            )


def shards(control, perturbation, loc_row, loc_col, obs_tile, obs_count, obs_value):
    members, levels, rows, width = control.shape
    slabs = lax.axis_size("slab")
    groups = lax.axis_size("member")
    height = rows * slabs
    half = width // 2
    blocks = width // (2 * TILE)
    n_obs = obs_tile.shape[0]
    each = n_obs // blocks
    depth = levels * rows
    chunk = blocks // groups
    per_row = width // TILE
    mine = lax.axis_index("slab")
    assert slabs % blocks == 0 and blocks % groups == 0

    pairs = slabs // 2
    tiles = pl.pallas_call(
        functools.partial(tiles_kernel, slabs),
        in_specs=[VM],
        out_specs=VM,
        out_shape=jax.ShapeDtypeStruct((2, pairs, n_obs // TILE, TILE), jnp.int32),
        scratch_shapes=[pltpu.SemaphoreType.DMA((slabs,)), pltpu.SemaphoreType.DMA((slabs,))],
        compiler_params=pltpu.CompilerParams(collective_id=1, has_side_effects=True),
        name="tiles",
    )(obs_tile.reshape(-1, TILE))
    stack = members * each
    picked, value, seen = pl.pallas_call(
        functools.partial(pick_kernel, rows, per_row),
        grid=(blocks,),
        in_specs=[
            pl.BlockSpec((1, each, 1), lambda q: (q, 0, 0)),
            pl.BlockSpec((1, each, 1), lambda q: (q, 0, 0)),
            pl.BlockSpec((1, each, TILE), lambda q: (q, 0, 0)),
            pl.BlockSpec((members, levels, rows, 2 * TILE), lambda q: (0, 0, 0, q)),
        ],
        out_specs=[
            pl.BlockSpec((stack, TILE), lambda q: (q, 0)),
            pl.BlockSpec((1, each, TILE), lambda q: (q, 0, 0)),
            pl.BlockSpec((1, each, TILE), lambda q: (q, 0, 0)),
        ],
        out_shape=[
            jax.ShapeDtypeStruct((blocks * stack, TILE), BF),
            jax.ShapeDtypeStruct((blocks, each, TILE), F32),
            jax.ShapeDtypeStruct((blocks, each, TILE), F32),
        ],
        name="pick",
    )(
        obs_tile.reshape(blocks, each, 1),
        obs_count.reshape(blocks, each, 1),
        obs_value.reshape(blocks, each, TILE),
        perturbation,
    )
    pieces = [picked]
    for i in range(1, pairs):
        ring = [(k, (k + 2 * i) % slabs) for k in range(slabs)]
        pieces.append(lax.ppermute(picked, "slab", ring))

    column = jnp.arange(half, dtype=jnp.int32)
    swapped = column - column % TILE + (column % TILE + HALF) % TILE
    table_even = column_table(2 * column, width, half)
    table_odd = column_table(2 * swapped + 1, width, half)

    row_col = loc_row[:, :, None]
    table_spec = pl.BlockSpec((half, half), lambda m: (0, 0))
    row_spec = pl.BlockSpec((levels, rows, 1), lambda m: (0, 0, 0))
    col_spec = pl.BlockSpec((levels, width), lambda m: (0, 0))
    big_spec = pl.BlockSpec((1, levels, rows, width), lambda m: (m, 0, 0, 0))
    half_spec = pl.BlockSpec((blocks, depth, 2 * TILE), lambda m: (0, m, 0))
    half_shape = jax.ShapeDtypeStruct((blocks, members * depth, 2 * TILE), BF)
    flops = 4 * members * depth * half * half
    along = pl.pallas_call(
        along_kernel,
        grid=(members,),
        in_specs=[big_spec, row_spec, col_spec, table_spec, table_spec],
        out_specs=half_spec,
        out_shape=half_shape,
        cost_estimate=pl.CostEstimate(flops=flops, bytes_accessed=16 << 20, transcendentals=0),
        name="along",
    )(control, row_col, loc_col, table_even, table_odd)

    e = jnp.arange(2, dtype=jnp.int32)[:, None]
    i = jnp.arange(pairs, dtype=jnp.int32)[None, :]
    source = (mine + e * (1 - 2 * (mine % 2)) - 2 * i) % slabs
    n = pairs * each
    listed = tiles.reshape(2, pairs, blocks, each)
    row_of = source[:, :, None, None] * rows + listed // per_row % rows
    code_of = listed // (rows * per_row) * 2 + listed % 2
    y = jnp.transpose(row_of, (2, 0, 1, 3)).reshape(blocks, 2, n, 1)
    code = jnp.transpose(code_of, (2, 0, 1, 3)).reshape(blocks, 2, n, 1)
    a = mine * rows + jnp.arange(rows, dtype=jnp.int32)
    ch, sh = turn(y * a, height)
    table_h = ((ch + sh) * (1.0 / math.sqrt(height))).astype(BF)

    n_copies = pairs + 2 * (groups + slabs - 2)
    back = pl.pallas_call(
        functools.partial(core_kernel, members, levels, groups, slabs),
        in_specs=[VM] * (5 + pairs),
        out_specs=VM,
        out_shape=half_shape,
        scratch_shapes=[
            pltpu.VMEM((pairs, blocks * stack, TILE), BF),
            pltpu.VMEM((blocks, 2, pairs, each, TILE), BF),
            pltpu.VMEM((groups - 1, chunk, 2, pairs, each, TILE), BF),
            pltpu.VMEM((2, pairs, chunk, each, TILE), BF),
            pltpu.VMEM((slabs - 1, chunk, each, TILE), BF),
            pltpu.VMEM((chunk, each, TILE), BF),
            pltpu.VMEM((2, pairs, chunk, each, TILE), BF),
            pltpu.VMEM((groups - 1, 2, pairs, chunk, each, TILE), BF),
            pltpu.SemaphoreType.DMA((n_copies,)),
            pltpu.SemaphoreType.DMA((n_copies,)),
        ],
        compiler_params=pltpu.CompilerParams(collective_id=0, has_side_effects=True),
        name="core",
    )(table_h, code, along, value, seen, *pieces)

    return pl.pallas_call(
        gradient_kernel,
        grid=(members,),
        in_specs=[half_spec, row_spec, col_spec, table_spec, table_spec],
        out_specs=big_spec,
        out_shape=jax.ShapeDtypeStruct(control.shape, F32),
        cost_estimate=pl.CostEstimate(flops=flops, bytes_accessed=16 << 20, transcendentals=0),
        name="gradient",
    )(back, row_col, loc_col, table_even, table_odd)


def solution(mesh):
    placed = (
        P("member", None, "slab", None),
        P("member", None, "slab", None),
        P(None, "slab"),
        P(),
        P("slab"),
        P("slab"),
        P("slab", None),
    )
    return jax.shard_map(
        shards,
        mesh=mesh,
        in_specs=placed,
        out_specs=P("member", None, "slab", None),
        check_vma=False,
    )
```

```python
import functools
import math

import jax
import jax.numpy as jnp
from jax import lax
from jax.experimental import pallas as pl
from jax.experimental.pallas import tpu as pltpu
from jax.sharding import PartitionSpec as P

TILE = 128
HALF = TILE // 2
BF = jnp.bfloat16
F32 = jnp.float32
MESH = pl.DeviceIdType.MESH
VM = pl.BlockSpec(memory_space=pltpu.VMEM)


def turn(product, order):
    angle = (2.0 * math.pi / order) * (product % order).astype(F32)
    return jnp.cos(angle), jnp.sin(angle)


def column_table(column, order, depth):
    step = 32
    outer = jnp.arange(depth // step, dtype=jnp.int32)[:, None] * step
    inner = jnp.arange(step, dtype=jnp.int32)[:, None]
    ca, sa = turn(outer * column[None, :], order)
    cb, sb = turn(inner * column[None, :], order)
    scale = 1.0 / math.sqrt(order)
    plus, minus = (cb + sb) * scale, (cb - sb) * scale
    table = ca[:, None, :] * plus[None] + sa[:, None, :] * minus[None]
    return table.astype(BF).reshape(depth, column.shape[0])


def low_half(shape):
    return lax.broadcasted_iota(jnp.int32, shape, 1) < HALF


def cell_of_lane(lane, parity):
    high = (lane >= HALF).astype(jnp.int32)
    return 2 * (lane - HALF * high) + jnp.where(parity == 0, high, 1 - high)


def pick_kernel(rows, per_row, each, tile_ref, count_ref, value_ref, pert_ref, pert_out, value_out, seen_out):
    members, levels = pert_ref.shape[:2]
    depth = levels * rows
    step = pl.program_id(0)

    def down(ref):
        return jnp.broadcast_to(ref[pl.ds(step, 1), :].astype(F32), (TILE, TILE)).T.astype(jnp.int32)

    tile = down(tile_ref)
    level_row = tile // per_row
    parity = tile % 2
    lane = lax.broadcasted_iota(jnp.int32, (TILE, TILE), 1)
    cell = lax.broadcasted_iota(jnp.int32, (TILE, TILE), 0)
    hot = jnp.concatenate([(lane + k == level_row).astype(F32) for k in range(0, depth, TILE)], 1).astype(BF)
    move0 = (cell == cell_of_lane(lane, 0)).astype(F32)
    move1 = (cell == cell_of_lane(lane, 1)).astype(F32)
    low0, low1 = move0.astype(BF), move1.astype(BF)
    for u in range(TILE // each):
        mine = slice(u * each, (u + 1) * each)
        both = []
        for m in range(members):
            block = pert_ref[m, :, :, 2 * TILE * u : 2 * TILE * (u + 1)].reshape(depth, 2 * TILE)
            both.append(jnp.dot(hot[mine], block, preferred_element_type=F32).astype(BF))
        both = jnp.concatenate(both, 0)
        first = jnp.dot(both[:, :TILE], low0, preferred_element_type=F32)
        second = jnp.dot(both[:, TILE:], low1, preferred_element_type=F32)
        even = jnp.concatenate([parity[mine]] * members, 0) == 0
        stack = members * each
        pert_out[u * stack : (u + 1) * stack, :] = jnp.where(even, first, second).astype(BF)
    value = value_ref[...]
    first = jnp.dot(value, move0, precision=lax.Precision.HIGHEST, preferred_element_type=F32)
    second = jnp.dot(value, move1, precision=lax.Precision.HIGHEST, preferred_element_type=F32)
    value_out[...] = jnp.where(parity == 0, first, second)
    seen_out[...] = (cell_of_lane(lane, parity) < down(count_ref)).astype(F32)


def along_kernel(control_ref, row_ref, col_ref, even_ref, odd_ref, out_ref):
    levels, rows, width = control_ref.shape[1:]
    half = width // 2
    plus, minus = [], []
    for l in range(levels):
        row = row_ref[l]
        a = control_ref[0, l, :, :half] * (row * col_ref[l : l + 1, :half])
        b = control_ref[0, l, :, half:] * (row * col_ref[l : l + 1, half:])
        plus.append((a + b).astype(BF))
        minus.append((a - b).astype(BF))
    plus = jnp.concatenate(plus, 0)
    minus = jnp.concatenate(minus, 0)
    even = jnp.dot(plus, even_ref[...], preferred_element_type=F32).astype(BF)
    odd = jnp.dot(minus, odd_ref[...], preferred_element_type=F32).astype(BF)
    for q in range(out_ref.shape[0]):
        out_ref[q, :, :TILE] = even[:, q * TILE : (q + 1) * TILE]
        out_ref[q, :, TILE:] = odd[:, q * TILE : (q + 1) * TILE]


def by_level(table, level, levels):
    return jnp.concatenate([jnp.where(level == l, table, jnp.zeros_like(table)) for l in range(levels)], 1)


def other_core(index, e):
    return index + e * (1 - 2 * lax.rem(index, 2))


def tiles_kernel(slabs, tile_ref, out_ref, send, recv):
    r = lax.axis_index("member")
    s = lax.axis_index("slab")
    barrier = pltpu.get_barrier_semaphore()
    for d in range(1, slabs):
        pl.semaphore_signal(barrier, inc=1, device_id=(r, lax.rem(s + d, slabs)), device_id_type=MESH)
    pl.semaphore_wait(barrier, slabs - 1)
    copies = []
    for k in range(1, slabs):
        e, i = k % 2, k // 2
        c = pltpu.make_async_remote_copy(
            src_ref=tile_ref, dst_ref=out_ref.at[e, i], send_sem=send.at[k], recv_sem=recv.at[k],
            device_id=(r, other_core(lax.rem(s + 2 * i, slabs), e)), device_id_type=MESH,
        )
        c.start()
        copies.append(c)
    out_ref[0, 0] = tile_ref[...]
    for c in copies:
        c.wait()


def core_kernel(members, levels, groups, slabs, h_ref, code_ref, along_ref, value_ref, seen_ref, *rest):
    pairs = slabs // 2
    pieces, rest = rest[:pairs], rest[pairs:]
    back_ref, swapped, part, land_a, pack_b, land_b, mine_c, land_c, land_d, send, recv = rest
    r = lax.axis_index("member")
    s = lax.axis_index("slab")
    blocks, _, n, _ = h_ref.shape
    chunk = blocks // groups
    depth = along_ref.shape[1] // members
    each = n // pairs
    stack = members * each
    barrier = pltpu.get_barrier_semaphore()
    for d in range(1, groups):
        pl.semaphore_signal(barrier, inc=1, device_id=(lax.rem(r + d, groups), s), device_id_type=MESH)
    for d in range(1, slabs):
        pl.semaphore_signal(barrier, inc=1, device_id=(r, lax.rem(s + d, slabs)), device_id_type=MESH)
    pl.semaphore_wait(barrier, groups + slabs - 2)
    used = [0]

    def copy(src, dst, where):
        k = used[0]
        used[0] += 1
        c = pltpu.make_async_remote_copy(
            src_ref=src, dst_ref=dst, send_sem=send.at[k], recv_sem=recv.at[k],
            device_id=where, device_id_type=MESH,
        )
        c.start()
        return c

    swaps = [copy(pieces[i], swapped.at[i], (r, other_core(s, 1))) for i in range(pairs)]

    def pert_rows(q, e, m):
        at = pl.ds(pl.multiple_of(q * stack + m * each, each), each)
        rows = [swapped[i, at, :] if e else pieces[i][at, :] for i in range(pairs)]
        return jnp.concatenate(rows, 0).astype(F32)

    def forward(q, e):
        code = code_ref[q, e]
        hm = by_level(h_ref[q, e], code // 2, levels)
        straight = low_half((n, TILE)) == (code % 2 == 0)
        acc = jnp.zeros((n, TILE), F32)
        for m in range(members):
            fg = jnp.dot(hm, along_ref[q, m * depth : (m + 1) * depth, :], preferred_element_type=F32)
            acc += pert_rows(q, e, m) * jnp.where(straight, fg[:, :TILE], fg[:, TILE:])
        part[q, e] = acc.astype(BF).reshape(pairs, each, TILE)

    @pl.loop(0, blocks)
    def _(q):
        forward(q, 0)

    for c in swaps:
        c.wait()
    copies = []
    for d in list(range(1, groups)) + [0]:
        to = lax.rem(r + d, groups)

        @pl.loop(0, chunk)
        def _(u):
            forward(to * chunk + u, 1)

        if d:
            copies.append(copy(part.at[pl.ds(to * chunk, chunk)], land_a.at[d - 1], (to, s)))

    total = part[pl.ds(r * chunk, chunk)].astype(F32)
    for d, c in enumerate(copies):
        c.wait()
        total += land_a[d].astype(F32)
    for e in range(2):
        for i in range(pairs):
            pack_b[e, i] = total[:, e, i].astype(BF)
    cells = total[:, 0, 0]
    copies = []
    for k in range(1, slabs):
        e, i = k % 2, k // 2
        to = other_core(lax.rem(s + slabs - 2 * i, slabs), e)
        copies.append(copy(pack_b.at[e, i], land_b.at[k - 1], (r, to)))
    for k, c in enumerate(copies):
        c.wait()
        cells += land_b[k].astype(F32)
    resid = cells - value_ref[pl.ds(r * chunk, chunk)]
    score = resid / jnp.sqrt(1.0 + resid * resid / 4.0)
    score = jnp.where(seen_ref[pl.ds(r * chunk, chunk)] > 0.5, score, 0.0).astype(BF)
    mine_c[...] = score
    land_c[0, 0] = score
    copies = []
    for k in range(1, slabs):
        e, i = k % 2, k // 2
        to = other_core(lax.rem(s + 2 * i, slabs), e)
        copies.append(copy(mine_c, land_c.at[e, i], (r, to)))
    spread = [[] for _ in range(groups)]

    def hand_on(src, e, i):
        for d in range(1, groups):
            spread[d].append(copy(src, land_d.at[d - 1, e, i], (lax.rem(r + d, groups), s)))

    hand_on(mine_c, 0, 0)
    for k in range(1, slabs):
        e, i = k % 2, k // 2
        copies[k - 1].wait()
        hand_on(land_c.at[e, i], e, i)
    over = (((0,), (0,)), ((), ()))

    def backward(q, read):
        hm = jnp.concatenate([by_level(h_ref[q, e], code_ref[q, e] // 2, levels) for e in range(2)], 0)
        code = jnp.concatenate([code_ref[q, 0], code_ref[q, 1]], 0)
        straight = low_half((2 * n, TILE)) == (code % 2 == 0)
        score = jnp.concatenate([read(e, i) for e in range(2) for i in range(pairs)], 0).astype(F32)
        both = []
        for m in range(members):
            w = jnp.concatenate([pert_rows(q, 0, m), pert_rows(q, 1, m)], 0) * score
            both += [jnp.where(straight, w, 0.0).astype(BF), jnp.where(straight, 0.0, w).astype(BF)]
        out = lax.dot_general(hm, jnp.concatenate(both, 1), over, preferred_element_type=F32).astype(BF)
        for m in range(members):
            back_ref[q, m * depth : (m + 1) * depth, :] = out[:, 2 * TILE * m : 2 * TILE * (m + 1)]

    @pl.loop(0, chunk)
    def _(u):
        backward(r * chunk + u, lambda e, i: land_c[e, i, u])

    for d in range(1, groups):
        for c in spread[groups - d]:
            c.wait()
        source = lax.rem(r + d, groups)

        @pl.loop(0, chunk)
        def _(u):
            backward(source * chunk + u, lambda e, i: land_d[groups - 1 - d, e, i, u])


def gradient_kernel(back_ref, row_ref, col_ref, even_ref, odd_ref, out_ref):
    levels, rows, width = out_ref.shape[1:]
    half = width // 2
    over = (((1,), (1,)), ((), ()))
    chunk = 512
    blocks = back_ref.shape[0]
    ev = jnp.concatenate([back_ref[q, :, :TILE] for q in range(blocks)], 1)
    od = jnp.concatenate([back_ref[q, :, TILE:] for q in range(blocks)], 1)
    for c in range(0, half, chunk):
        e = lax.dot_general(ev, even_ref[c : c + chunk, :], over, preferred_element_type=F32)
        o = lax.dot_general(od, odd_ref[c : c + chunk, :], over, preferred_element_type=F32)
        for l in range(levels):
            el, ol = e[l * rows : (l + 1) * rows], o[l * rows : (l + 1) * rows]
            row = row_ref[l]
            out_ref[0, l, :, c : c + chunk] = (el + ol) * (row * col_ref[l : l + 1, c : c + chunk])
            out_ref[0, l, :, half + c : half + c + chunk] = (el - ol) * (
                row * col_ref[l : l + 1, half + c : half + c + chunk]
            )


def shards(control, perturbation, loc_row, loc_col, obs_tile, obs_count, obs_value):
    members, levels, rows, width = control.shape
    slabs = lax.axis_size("slab")
    groups = lax.axis_size("member")
    height = rows * slabs
    half = width // 2
    blocks = width // (2 * TILE)
    n_obs = obs_tile.shape[0]
    each = n_obs // blocks
    depth = levels * rows
    chunk = blocks // groups
    per_row = width // TILE
    mine = lax.axis_index("slab")
    assert slabs % blocks == 0 and blocks % groups == 0

    pairs = slabs // 2
    tiles = pl.pallas_call(
        functools.partial(tiles_kernel, slabs),
        in_specs=[VM],
        out_specs=VM,
        out_shape=jax.ShapeDtypeStruct((2, pairs, n_obs // TILE, TILE), jnp.int32),
        scratch_shapes=[pltpu.SemaphoreType.DMA((slabs,)), pltpu.SemaphoreType.DMA((slabs,))],
        compiler_params=pltpu.CompilerParams(collective_id=1, has_side_effects=True),
        name="tiles",
    )(obs_tile.reshape(-1, TILE))
    stack = members * each
    steps = n_obs // TILE
    cut = TILE // each
    flat_spec = pl.BlockSpec((steps, TILE), lambda g: (0, 0))
    cell_spec = pl.BlockSpec((TILE, TILE), lambda g: (g, 0))
    cell_shape = jax.ShapeDtypeStruct((n_obs, TILE), F32)
    picked, value, seen = pl.pallas_call(
        functools.partial(pick_kernel, rows, per_row, each),
        grid=(steps,),
        in_specs=[
            flat_spec,
            flat_spec,
            cell_spec,
            pl.BlockSpec((members, levels, rows, 2 * TILE * cut), lambda g: (0, 0, 0, g)),
        ],
        out_specs=[pl.BlockSpec((cut * stack, TILE), lambda g: (g, 0)), cell_spec, cell_spec],
        out_shape=[jax.ShapeDtypeStruct((blocks * stack, TILE), BF), cell_shape, cell_shape],
        name="pick",
    )(tiles[0, 0], obs_count.reshape(steps, TILE), obs_value, perturbation)
    value = value.reshape(blocks, each, TILE)
    seen = seen.reshape(blocks, each, TILE)
    pieces = [picked]
    for i in range(1, pairs):
        ring = [(k, (k + 2 * i) % slabs) for k in range(slabs)]
        pieces.append(lax.ppermute(picked, "slab", ring))

    column = jnp.arange(half, dtype=jnp.int32)
    swapped = column - column % TILE + (column % TILE + HALF) % TILE
    table_even = column_table(2 * column, width, half)
    table_odd = column_table(2 * swapped + 1, width, half)

    row_col = loc_row[:, :, None]
    table_spec = pl.BlockSpec((half, half), lambda m: (0, 0))
    row_spec = pl.BlockSpec((levels, rows, 1), lambda m: (0, 0, 0))
    col_spec = pl.BlockSpec((levels, width), lambda m: (0, 0))
    big_spec = pl.BlockSpec((1, levels, rows, width), lambda m: (m, 0, 0, 0))
    half_spec = pl.BlockSpec((blocks, depth, 2 * TILE), lambda m: (0, m, 0))
    half_shape = jax.ShapeDtypeStruct((blocks, members * depth, 2 * TILE), BF)
    flops = 4 * members * depth * half * half
    along = pl.pallas_call(
        along_kernel,
        grid=(members,),
        in_specs=[big_spec, row_spec, col_spec, table_spec, table_spec],
        out_specs=half_spec,
        out_shape=half_shape,
        cost_estimate=pl.CostEstimate(flops=flops, bytes_accessed=16 << 20, transcendentals=0),
        name="along",
    )(control, row_col, loc_col, table_even, table_odd)

    e = jnp.arange(2, dtype=jnp.int32)[:, None]
    i = jnp.arange(pairs, dtype=jnp.int32)[None, :]
    source = (mine + e * (1 - 2 * (mine % 2)) - 2 * i) % slabs
    n = pairs * each
    listed = tiles.reshape(2, pairs, blocks, each)
    row_of = source[:, :, None, None] * rows + listed // per_row % rows
    code_of = listed // (rows * per_row) * 2 + listed % 2
    y = jnp.transpose(row_of, (2, 0, 1, 3)).reshape(blocks, 2, n, 1)
    code = jnp.transpose(code_of, (2, 0, 1, 3)).reshape(blocks, 2, n, 1)
    a = mine * rows + jnp.arange(rows, dtype=jnp.int32)
    ch, sh = turn(y * a, height)
    table_h = ((ch + sh) * (1.0 / math.sqrt(height))).astype(BF)

    n_copies = pairs + 2 * (slabs - 1) + (groups - 1) * (slabs + 1)
    back = pl.pallas_call(
        functools.partial(core_kernel, members, levels, groups, slabs),
        in_specs=[VM] * (5 + pairs),
        out_specs=VM,
        out_shape=half_shape,
        scratch_shapes=[
            pltpu.VMEM((pairs, blocks * stack, TILE), BF),
            pltpu.VMEM((blocks, 2, pairs, each, TILE), BF),
            pltpu.VMEM((groups - 1, chunk, 2, pairs, each, TILE), BF),
            pltpu.VMEM((2, pairs, chunk, each, TILE), BF),
            pltpu.VMEM((slabs - 1, chunk, each, TILE), BF),
            pltpu.VMEM((chunk, each, TILE), BF),
            pltpu.VMEM((2, pairs, chunk, each, TILE), BF),
            pltpu.VMEM((groups - 1, 2, pairs, chunk, each, TILE), BF),
            pltpu.SemaphoreType.DMA((n_copies,)),
            pltpu.SemaphoreType.DMA((n_copies,)),
        ],
        compiler_params=pltpu.CompilerParams(collective_id=0, has_side_effects=True),
        name="core",
    )(table_h, code, along, value, seen, *pieces)

    return pl.pallas_call(
        gradient_kernel,
        grid=(members,),
        in_specs=[half_spec, row_spec, col_spec, table_spec, table_spec],
        out_specs=big_spec,
        out_shape=jax.ShapeDtypeStruct(control.shape, F32),
        cost_estimate=pl.CostEstimate(flops=flops, bytes_accessed=16 << 20, transcendentals=0),
        name="gradient",
    )(back, row_col, loc_col, table_even, table_odd)


def solution(mesh):
    placed = (
        P("member", None, "slab", None),
        P("member", None, "slab", None),
        P(None, "slab"),
        P(),
        P("slab"),
        P("slab"),
        P("slab", None),
    )
    return jax.shard_map(
        shards,
        mesh=mesh,
        in_specs=placed,
        out_specs=P("member", None, "slab", None),
        check_vma=False,
    )
```

```python
import functools
import math

import jax
import jax.numpy as jnp
from jax import lax
from jax.experimental import pallas as pl
from jax.experimental.pallas import tpu as pltpu
from jax.sharding import PartitionSpec as P

TILE = 128
HALF = TILE // 2
BF = jnp.bfloat16
F32 = jnp.float32
MESH = pl.DeviceIdType.MESH
VM = pl.BlockSpec(memory_space=pltpu.VMEM)


def turn(product, order):
    angle = (2.0 * math.pi / order) * (product % order).astype(F32)
    return jnp.cos(angle), jnp.sin(angle)


def column_table(column, order, depth):
    step = 32
    outer = jnp.arange(depth // step, dtype=jnp.int32)[:, None] * step
    inner = jnp.arange(step, dtype=jnp.int32)[:, None]
    ca, sa = turn(outer * column[None, :], order)
    cb, sb = turn(inner * column[None, :], order)
    scale = 1.0 / math.sqrt(order)
    plus, minus = (cb + sb) * scale, (cb - sb) * scale
    table = ca[:, None, :] * plus[None] + sa[:, None, :] * minus[None]
    return table.astype(BF).reshape(depth, column.shape[0])


def low_half(shape):
    return lax.broadcasted_iota(jnp.int32, shape, 1) < HALF


def cell_of_lane(lane, parity):
    high = (lane >= HALF).astype(jnp.int32)
    return 2 * (lane - HALF * high) + jnp.where(parity == 0, high, 1 - high)


def pick_kernel(rows, per_row, each, tile_ref, count_ref, value_ref, pert_ref, pert_out, value_out, seen_out):
    members, levels = pert_ref.shape[:2]
    depth = levels * rows
    step = pl.program_id(0)

    def down(ref):
        return jnp.broadcast_to(ref[pl.ds(step, 1), :].astype(F32), (TILE, TILE)).T.astype(jnp.int32)

    tile = down(tile_ref)
    level_row = tile // per_row
    parity = tile % 2
    lane = lax.broadcasted_iota(jnp.int32, (TILE, TILE), 1)
    cell = lax.broadcasted_iota(jnp.int32, (TILE, TILE), 0)
    hot = jnp.concatenate([(lane + k == level_row).astype(F32) for k in range(0, depth, TILE)], 1).astype(BF)
    move0 = (cell == cell_of_lane(lane, 0)).astype(F32)
    move1 = (cell == cell_of_lane(lane, 1)).astype(F32)
    low0, low1 = move0.astype(BF), move1.astype(BF)
    for u in range(TILE // each):
        mine = slice(u * each, (u + 1) * each)
        both = []
        for m in range(members):
            block = pert_ref[m, :, :, 2 * TILE * u : 2 * TILE * (u + 1)].reshape(depth, 2 * TILE)
            both.append(jnp.dot(hot[mine], block, preferred_element_type=F32).astype(BF))
        both = jnp.concatenate(both, 0)
        first = jnp.dot(both[:, :TILE], low0, preferred_element_type=F32)
        second = jnp.dot(both[:, TILE:], low1, preferred_element_type=F32)
        even = jnp.concatenate([parity[mine]] * members, 0) == 0
        stack = members * each
        pert_out[u * stack : (u + 1) * stack, :] = jnp.where(even, first, second).astype(BF)
    value = value_ref[...]
    first = jnp.dot(value, move0, precision=lax.Precision.HIGHEST, preferred_element_type=F32)
    second = jnp.dot(value, move1, precision=lax.Precision.HIGHEST, preferred_element_type=F32)
    value_out[...] = jnp.where(parity == 0, first, second)
    seen_out[...] = (cell_of_lane(lane, parity) < down(count_ref)).astype(F32)


def along_kernel(control_ref, row_ref, col_ref, even_ref, odd_ref, out_ref):
    levels, rows, width = control_ref.shape[1:]
    half = width // 2
    plus, minus = [], []
    for l in range(levels):
        row = row_ref[l]
        a = control_ref[0, l, :, :half] * (row * col_ref[l : l + 1, :half])
        b = control_ref[0, l, :, half:] * (row * col_ref[l : l + 1, half:])
        plus.append((a + b).astype(BF))
        minus.append((a - b).astype(BF))
    plus = jnp.concatenate(plus, 0)
    minus = jnp.concatenate(minus, 0)
    even = jnp.dot(plus, even_ref[...], preferred_element_type=F32).astype(BF)
    odd = jnp.dot(minus, odd_ref[...], preferred_element_type=F32).astype(BF)
    for q in range(out_ref.shape[0]):
        out_ref[q, :, :TILE] = even[:, q * TILE : (q + 1) * TILE]
        out_ref[q, :, TILE:] = odd[:, q * TILE : (q + 1) * TILE]


def by_level(table, level, levels):
    return jnp.concatenate([jnp.where(level == l, table, jnp.zeros_like(table)) for l in range(levels)], 1)


def other_core(index, e):
    return index + e * (1 - 2 * lax.rem(index, 2))


def tiles_kernel(slabs, tile_ref, out_ref, send, recv):
    r = lax.axis_index("member")
    s = lax.axis_index("slab")
    barrier = pltpu.get_barrier_semaphore()
    for d in range(1, slabs):
        pl.semaphore_signal(barrier, inc=1, device_id=(r, lax.rem(s + d, slabs)), device_id_type=MESH)
    pl.semaphore_wait(barrier, slabs - 1)
    copies = []
    for k in range(1, slabs):
        e, i = k % 2, k // 2
        c = pltpu.make_async_remote_copy(
            src_ref=tile_ref, dst_ref=out_ref.at[e, i], send_sem=send.at[k], recv_sem=recv.at[k],
            device_id=(r, other_core(lax.rem(s + 2 * i, slabs), e)), device_id_type=MESH,
        )
        c.start()
        copies.append(c)
    out_ref[0, 0] = tile_ref[...]
    for c in copies:
        c.wait()


def core_kernel(members, levels, groups, slabs, h_ref, code_ref, along_ref, value_ref, seen_ref, *rest):
    pairs = slabs // 2
    pieces, rest = rest[:pairs], rest[pairs:]
    back_ref, swapped, part, land_a, pack_b, land_b, mine_c, land_c, land_d, send, recv = rest
    r = lax.axis_index("member")
    s = lax.axis_index("slab")
    blocks, _, n, _ = h_ref.shape
    chunk = blocks // groups
    depth = along_ref.shape[1] // members
    each = n // pairs
    stack = members * each
    barrier = pltpu.get_barrier_semaphore()
    for d in range(1, groups):
        pl.semaphore_signal(barrier, inc=1, device_id=(lax.rem(r + d, groups), s), device_id_type=MESH)
    for d in range(1, slabs):
        pl.semaphore_signal(barrier, inc=1, device_id=(r, lax.rem(s + d, slabs)), device_id_type=MESH)
    pl.semaphore_wait(barrier, groups + slabs - 2)
    used = [0]

    def copy(src, dst, where):
        k = used[0]
        used[0] += 1
        c = pltpu.make_async_remote_copy(
            src_ref=src, dst_ref=dst, send_sem=send.at[k], recv_sem=recv.at[k],
            device_id=where, device_id_type=MESH,
        )
        c.start()
        return c

    swaps = [copy(pieces[i], swapped.at[i], (r, other_core(s, 1))) for i in range(pairs)]

    def pert_rows(q, e, m):
        at = pl.ds(pl.multiple_of(q * stack + m * each, each), each)
        rows = [swapped[i, at, :] if e else pieces[i][at, :] for i in range(pairs)]
        return jnp.concatenate(rows, 0).astype(F32)

    def forward(q, e):
        code = code_ref[q, e]
        hm = by_level(h_ref[q, e], code // 2, levels)
        straight = low_half((n, TILE)) == (code % 2 == 0)
        acc = jnp.zeros((n, TILE), F32)
        for m in range(members):
            fg = jnp.dot(hm, along_ref[q, m * depth : (m + 1) * depth, :], preferred_element_type=F32)
            acc += pert_rows(q, e, m) * jnp.where(straight, fg[:, :TILE], fg[:, TILE:])
        part[q, e] = acc.astype(BF).reshape(pairs, each, TILE)

    @pl.loop(0, blocks)
    def _(q):
        forward(q, 0)

    for c in swaps:
        c.wait()
    copies = []
    for d in list(range(1, groups)) + [0]:
        to = lax.rem(r + d, groups)

        @pl.loop(0, chunk)
        def _(u):
            forward(to * chunk + u, 1)

        if d:
            copies.append(copy(part.at[pl.ds(to * chunk, chunk)], land_a.at[d - 1], (to, s)))

    total = part[pl.ds(r * chunk, chunk)].astype(F32)
    for d, c in enumerate(copies):
        c.wait()
        total += land_a[d].astype(F32)
    for e in range(2):
        for i in range(pairs):
            pack_b[e, i] = total[:, e, i].astype(BF)
    cells = total[:, 0, 0]
    copies = []
    for k in range(1, slabs):
        e, i = k % 2, k // 2
        to = other_core(lax.rem(s + slabs - 2 * i, slabs), e)
        copies.append(copy(pack_b.at[e, i], land_b.at[k - 1], (r, to)))
    for k, c in enumerate(copies):
        c.wait()
        cells += land_b[k].astype(F32)
    resid = cells - value_ref[pl.ds(r * chunk, chunk)]
    score = resid / jnp.sqrt(1.0 + resid * resid / 4.0)
    score = jnp.where(seen_ref[pl.ds(r * chunk, chunk)] > 0.5, score, 0.0).astype(BF)
    mine_c[...] = score
    land_c[0, 0] = score
    copies = []
    for k in range(1, slabs):
        e, i = k % 2, k // 2
        to = other_core(lax.rem(s + 2 * i, slabs), e)
        copies.append(copy(mine_c, land_c.at[e, i], (r, to)))
    spread = [[] for _ in range(groups)]

    def hand_on(src, e, i):
        for d in range(1, groups):
            spread[d].append(copy(src, land_d.at[d - 1, e, i], (lax.rem(r + d, groups), s)))

    hand_on(mine_c, 0, 0)
    for k in range(1, slabs):
        e, i = k % 2, k // 2
        copies[k - 1].wait()
        hand_on(land_c.at[e, i], e, i)
    over = (((0,), (0,)), ((), ()))

    def backward(q, read):
        hm = jnp.concatenate([by_level(h_ref[q, e], code_ref[q, e] // 2, levels) for e in range(2)], 0)
        code = jnp.concatenate([code_ref[q, 0], code_ref[q, 1]], 0)
        straight = low_half((2 * n, TILE)) == (code % 2 == 0)
        score = jnp.concatenate([read(e, i) for e in range(2) for i in range(pairs)], 0).astype(F32)
        both = []
        for m in range(members):
            w = jnp.concatenate([pert_rows(q, 0, m), pert_rows(q, 1, m)], 0) * score
            both += [jnp.where(straight, w, 0.0).astype(BF), jnp.where(straight, 0.0, w).astype(BF)]
        out = lax.dot_general(hm, jnp.concatenate(both, 1), over, preferred_element_type=F32).astype(BF)
        for m in range(members):
            back_ref[q, m * depth : (m + 1) * depth, :] = out[:, 2 * TILE * m : 2 * TILE * (m + 1)]

    @pl.loop(0, chunk)
    def _(u):
        backward(r * chunk + u, lambda e, i: land_c[e, i, u])

    for d in range(1, groups):
        for c in spread[groups - d]:
            c.wait()
        source = lax.rem(r + d, groups)

        @pl.loop(0, chunk)
        def _(u):
            backward(source * chunk + u, lambda e, i: land_d[groups - 1 - d, e, i, u])


def gradient_kernel(back_ref, row_ref, col_ref, even_ref, odd_ref, out_ref):
    levels, rows, width = out_ref.shape[1:]
    half = width // 2
    over = (((1,), (1,)), ((), ()))
    chunk = 512
    blocks = back_ref.shape[0]
    ev = jnp.concatenate([back_ref[q, :, :TILE] for q in range(blocks)], 1)
    od = jnp.concatenate([back_ref[q, :, TILE:] for q in range(blocks)], 1)
    for c in range(0, half, chunk):
        e = lax.dot_general(ev, even_ref[c : c + chunk, :], over, preferred_element_type=F32)
        o = lax.dot_general(od, odd_ref[c : c + chunk, :], over, preferred_element_type=F32)
        for l in range(levels):
            el, ol = e[l * rows : (l + 1) * rows], o[l * rows : (l + 1) * rows]
            row = row_ref[l]
            out_ref[0, l, :, c : c + chunk] = (el + ol) * (row * col_ref[l : l + 1, c : c + chunk])
            out_ref[0, l, :, half + c : half + c + chunk] = (el - ol) * (
                row * col_ref[l : l + 1, half + c : half + c + chunk]
            )


def shards(control, perturbation, loc_row, loc_col, obs_tile, obs_count, obs_value):
    members, levels, rows, width = control.shape
    slabs = lax.axis_size("slab")
    groups = lax.axis_size("member")
    height = rows * slabs
    half = width // 2
    blocks = width // (2 * TILE)
    n_obs = obs_tile.shape[0]
    each = n_obs // blocks
    depth = levels * rows
    chunk = blocks // groups
    per_row = width // TILE
    mine = lax.axis_index("slab")
    assert slabs % blocks == 0 and blocks % groups == 0

    pairs = slabs // 2
    tiles = pl.pallas_call(
        functools.partial(tiles_kernel, slabs),
        in_specs=[VM],
        out_specs=VM,
        out_shape=jax.ShapeDtypeStruct((2, pairs, n_obs // TILE, TILE), jnp.int32),
        scratch_shapes=[pltpu.SemaphoreType.DMA((slabs,)), pltpu.SemaphoreType.DMA((slabs,))],
        compiler_params=pltpu.CompilerParams(collective_id=1, has_side_effects=True),
        name="tiles",
    )(obs_tile.reshape(-1, TILE))
    stack = members * each
    steps = n_obs // TILE
    cut = TILE // each
    flat_spec = pl.BlockSpec((steps, TILE), lambda g: (0, 0))
    cell_spec = pl.BlockSpec((TILE, TILE), lambda g: (g, 0))
    cell_shape = jax.ShapeDtypeStruct((n_obs, TILE), F32)
    picked, value, seen = pl.pallas_call(
        functools.partial(pick_kernel, rows, per_row, each),
        grid=(steps,),
        in_specs=[
            flat_spec,
            flat_spec,
            cell_spec,
            pl.BlockSpec((members, levels, rows, 2 * TILE * cut), lambda g: (0, 0, 0, g)),
        ],
        out_specs=[pl.BlockSpec((cut * stack, TILE), lambda g: (g, 0)), cell_spec, cell_spec],
        out_shape=[jax.ShapeDtypeStruct((blocks * stack, TILE), BF), cell_shape, cell_shape],
        name="pick",
    )(obs_tile.reshape(steps, TILE), obs_count.reshape(steps, TILE), obs_value, perturbation)
    picked, tiles = lax.optimization_barrier((picked, tiles))
    value = value.reshape(blocks, each, TILE)
    seen = seen.reshape(blocks, each, TILE)
    pieces = [picked]
    for i in range(1, pairs):
        ring = [(k, (k + 2 * i) % slabs) for k in range(slabs)]
        pieces.append(lax.ppermute(picked, "slab", ring))

    column = jnp.arange(half, dtype=jnp.int32)
    swapped = column - column % TILE + (column % TILE + HALF) % TILE
    table_even = column_table(2 * column, width, half)
    table_odd = column_table(2 * swapped + 1, width, half)

    row_col = loc_row[:, :, None]
    table_spec = pl.BlockSpec((half, half), lambda m: (0, 0))
    row_spec = pl.BlockSpec((levels, rows, 1), lambda m: (0, 0, 0))
    col_spec = pl.BlockSpec((levels, width), lambda m: (0, 0))
    big_spec = pl.BlockSpec((1, levels, rows, width), lambda m: (m, 0, 0, 0))
    half_spec = pl.BlockSpec((blocks, depth, 2 * TILE), lambda m: (0, m, 0))
    half_shape = jax.ShapeDtypeStruct((blocks, members * depth, 2 * TILE), BF)
    flops = 4 * members * depth * half * half
    along = pl.pallas_call(
        along_kernel,
        grid=(members,),
        in_specs=[big_spec, row_spec, col_spec, table_spec, table_spec],
        out_specs=half_spec,
        out_shape=half_shape,
        cost_estimate=pl.CostEstimate(flops=flops, bytes_accessed=16 << 20, transcendentals=0),
        compiler_params=pltpu.CompilerParams(vmem_limit_bytes=61 << 20),
        name="along",
    )(control, row_col, loc_col, table_even, table_odd)

    e = jnp.arange(2, dtype=jnp.int32)[:, None]
    i = jnp.arange(pairs, dtype=jnp.int32)[None, :]
    source = (mine + e * (1 - 2 * (mine % 2)) - 2 * i) % slabs
    n = pairs * each
    listed = tiles.reshape(2, pairs, blocks, each)
    row_of = source[:, :, None, None] * rows + listed // per_row % rows
    code_of = listed // (rows * per_row) * 2 + listed % 2
    y = jnp.transpose(row_of, (2, 0, 1, 3)).reshape(blocks, 2, n, 1)
    code = jnp.transpose(code_of, (2, 0, 1, 3)).reshape(blocks, 2, n, 1)
    a = mine * rows + jnp.arange(rows, dtype=jnp.int32)
    angle = (2.0 * math.pi / height) * (y * a % height).astype(F32) - math.pi / 4
    table_h = (jnp.cos(angle) * math.sqrt(2.0 / height)).astype(BF)

    n_copies = pairs + 2 * (slabs - 1) + (groups - 1) * (slabs + 1)
    back = pl.pallas_call(
        functools.partial(core_kernel, members, levels, groups, slabs),
        in_specs=[VM] * (5 + pairs),
        out_specs=VM,
        out_shape=half_shape,
        scratch_shapes=[
            pltpu.VMEM((pairs, blocks * stack, TILE), BF),
            pltpu.VMEM((blocks, 2, pairs, each, TILE), BF),
            pltpu.VMEM((groups - 1, chunk, 2, pairs, each, TILE), BF),
            pltpu.VMEM((2, pairs, chunk, each, TILE), BF),
            pltpu.VMEM((slabs - 1, chunk, each, TILE), BF),
            pltpu.VMEM((chunk, each, TILE), BF),
            pltpu.VMEM((2, pairs, chunk, each, TILE), BF),
            pltpu.VMEM((groups - 1, 2, pairs, chunk, each, TILE), BF),
            pltpu.SemaphoreType.DMA((n_copies,)),
            pltpu.SemaphoreType.DMA((n_copies,)),
        ],
        compiler_params=pltpu.CompilerParams(collective_id=0, has_side_effects=True, vmem_limit_bytes=40 << 20),
        name="core",
    )(table_h, code, along, value, seen, *pieces)

    return pl.pallas_call(
        gradient_kernel,
        grid=(members,),
        in_specs=[half_spec, row_spec, col_spec, table_spec, table_spec],
        out_specs=big_spec,
        out_shape=jax.ShapeDtypeStruct(control.shape, F32),
        cost_estimate=pl.CostEstimate(flops=flops, bytes_accessed=16 << 20, transcendentals=0),
        compiler_params=pltpu.CompilerParams(vmem_limit_bytes=24 << 20),
        name="gradient",
    )(back, row_col, loc_col, table_even, table_odd)


def solution(mesh):
    placed = (
        P("member", None, "slab", None),
        P("member", None, "slab", None),
        P(None, "slab"),
        P(),
        P("slab"),
        P("slab"),
        P("slab", None),
    )
    return jax.shard_map(
        shards,
        mesh=mesh,
        in_specs=placed,
        out_specs=P("member", None, "slab", None),
        check_vma=False,
    )
```

```python
import functools
import math

import jax
import jax.numpy as jnp
from jax import lax
from jax.experimental import pallas as pl
from jax.experimental.pallas import tpu as pltpu
from jax.sharding import PartitionSpec as P

TILE = 128
HALF = TILE // 2
BF = jnp.bfloat16
F32 = jnp.float32
MESH = pl.DeviceIdType.MESH
VM = pl.BlockSpec(memory_space=pltpu.VMEM)


def turn(product, order):
    angle = (2.0 * math.pi / order) * (product % order).astype(F32)
    return jnp.cos(angle), jnp.sin(angle)


def column_table(column, order, depth):
    step = 32
    outer = jnp.arange(depth // step, dtype=jnp.int32)[:, None] * step
    inner = jnp.arange(step, dtype=jnp.int32)[:, None]
    ca, sa = turn(outer * column[None, :], order)
    cb, sb = turn(inner * column[None, :], order)
    scale = 1.0 / math.sqrt(order)
    plus, minus = (cb + sb) * scale, (cb - sb) * scale
    table = ca[:, None, :] * plus[None] + sa[:, None, :] * minus[None]
    return table.astype(BF).reshape(depth, column.shape[0])


def low_half(shape):
    return lax.broadcasted_iota(jnp.int32, shape, 1) < HALF


def cell_of_lane(lane, parity):
    high = (lane >= HALF).astype(jnp.int32)
    return 2 * (lane - HALF * high) + jnp.where(parity == 0, high, 1 - high)


def pick_kernel(rows, per_row, each, tile_ref, count_ref, value_ref, pert_ref, pert_out, value_out, seen_out):
    members, levels = pert_ref.shape[:2]
    depth = levels * rows
    step = pl.program_id(0)

    def down(ref):
        return jnp.broadcast_to(ref[pl.ds(step, 1), :].astype(F32), (TILE, TILE)).T.astype(jnp.int32)

    tile = down(tile_ref)
    level_row = tile // per_row
    parity = tile % 2
    lane = lax.broadcasted_iota(jnp.int32, (TILE, TILE), 1)
    cell = lax.broadcasted_iota(jnp.int32, (TILE, TILE), 0)
    hot = jnp.concatenate([(lane + k == level_row).astype(F32) for k in range(0, depth, TILE)], 1).astype(BF)
    move0 = (cell == cell_of_lane(lane, 0)).astype(F32)
    move1 = (cell == cell_of_lane(lane, 1)).astype(F32)
    low0, low1 = move0.astype(BF), move1.astype(BF)
    for u in range(TILE // each):
        mine = slice(u * each, (u + 1) * each)
        both = []
        for m in range(members):
            block = pert_ref[m, :, :, 2 * TILE * u : 2 * TILE * (u + 1)].reshape(depth, 2 * TILE)
            both.append(jnp.dot(hot[mine], block, preferred_element_type=F32).astype(BF))
        both = jnp.concatenate(both, 0)
        first = jnp.dot(both[:, :TILE], low0, preferred_element_type=F32)
        second = jnp.dot(both[:, TILE:], low1, preferred_element_type=F32)
        even = jnp.concatenate([parity[mine]] * members, 0) == 0
        stack = members * each
        pert_out[u * stack : (u + 1) * stack, :] = jnp.where(even, first, second).astype(BF)
    value = value_ref[...]
    first = jnp.dot(value, move0, precision=lax.Precision.HIGHEST, preferred_element_type=F32)
    second = jnp.dot(value, move1, precision=lax.Precision.HIGHEST, preferred_element_type=F32)
    value_out[...] = jnp.where(parity == 0, first, second)
    seen_out[...] = (cell_of_lane(lane, parity) < down(count_ref)).astype(F32)


def along_kernel(control_ref, row_ref, col_ref, even_ref, odd_ref, out_ref):
    levels, rows, width = control_ref.shape[1:]
    half = width // 2
    plus, minus = [], []
    for l in range(levels):
        row = row_ref[l]
        a = control_ref[0, l, :, :half] * (row * col_ref[l : l + 1, :half])
        b = control_ref[0, l, :, half:] * (row * col_ref[l : l + 1, half:])
        plus.append((a + b).astype(BF))
        minus.append((a - b).astype(BF))
    plus = jnp.concatenate(plus, 0)
    minus = jnp.concatenate(minus, 0)
    even = jnp.dot(plus, even_ref[...], preferred_element_type=F32).astype(BF)
    odd = jnp.dot(minus, odd_ref[...], preferred_element_type=F32).astype(BF)
    for q in range(out_ref.shape[0]):
        out_ref[q, :, :TILE] = even[:, q * TILE : (q + 1) * TILE]
        out_ref[q, :, TILE:] = odd[:, q * TILE : (q + 1) * TILE]


def by_level(table, level, levels):
    return jnp.concatenate([jnp.where(level == l, table, jnp.zeros_like(table)) for l in range(levels)], 1)


def other_core(index, e):
    return index + e * (1 - 2 * lax.rem(index, 2))


def tiles_kernel(slabs, tile_ref, out_ref, send, recv):
    r = lax.axis_index("member")
    s = lax.axis_index("slab")
    barrier = pltpu.get_barrier_semaphore()
    for d in range(1, slabs):
        pl.semaphore_signal(barrier, inc=1, device_id=(r, lax.rem(s + d, slabs)), device_id_type=MESH)
    pl.semaphore_wait(barrier, slabs - 1)
    copies = []
    for k in range(1, slabs):
        e, i = k % 2, k // 2
        c = pltpu.make_async_remote_copy(
            src_ref=tile_ref, dst_ref=out_ref.at[e, i], send_sem=send.at[k], recv_sem=recv.at[k],
            device_id=(r, other_core(lax.rem(s + 2 * i, slabs), e)), device_id_type=MESH,
        )
        c.start()
        copies.append(c)
    out_ref[0, 0] = tile_ref[...]
    for c in copies:
        c.wait()


def core_kernel(members, levels, groups, slabs, h_ref, code_ref, along_ref, value_ref, seen_ref, *rest):
    pairs = slabs // 2
    pieces, rest = rest[:pairs], rest[pairs:]
    back_ref, swapped, part, land_a, pack_b, land_b, mine_c, land_c, land_d, send, recv = rest
    r = lax.axis_index("member")
    s = lax.axis_index("slab")
    blocks, _, n, _ = h_ref.shape
    chunk = blocks // groups
    depth = along_ref.shape[1] // members
    each = n // pairs
    stack = members * each
    barrier = pltpu.get_barrier_semaphore()
    for d in range(1, groups):
        pl.semaphore_signal(barrier, inc=1, device_id=(lax.rem(r + d, groups), s), device_id_type=MESH)
    for d in range(1, slabs):
        pl.semaphore_signal(barrier, inc=1, device_id=(r, lax.rem(s + d, slabs)), device_id_type=MESH)
    pl.semaphore_wait(barrier, groups + slabs - 2)
    used = [0]

    def copy(src, dst, where):
        k = used[0]
        used[0] += 1
        c = pltpu.make_async_remote_copy(
            src_ref=src, dst_ref=dst, send_sem=send.at[k], recv_sem=recv.at[k],
            device_id=where, device_id_type=MESH,
        )
        c.start()
        return c

    swaps = [copy(pieces[i], swapped.at[i], (r, other_core(s, 1))) for i in range(pairs)]

    def pert_rows(q, e, m):
        at = pl.ds(pl.multiple_of(q * stack + m * each, each), each)
        rows = [swapped[i, at, :] if e else pieces[i][at, :] for i in range(pairs)]
        return jnp.concatenate(rows, 0).astype(F32)

    def forward(q, e):
        code = code_ref[q, e]
        hm = by_level(h_ref[q, e], code // 2, levels)
        straight = low_half((n, TILE)) == (code % 2 == 0)
        acc = jnp.zeros((n, TILE), F32)
        for m in range(members):
            fg = jnp.dot(hm, along_ref[q, m * depth : (m + 1) * depth, :], preferred_element_type=F32)
            acc += pert_rows(q, e, m) * jnp.where(straight, fg[:, :TILE], fg[:, TILE:])
        part[q, e] = acc.astype(BF).reshape(pairs, each, TILE)

    @pl.loop(0, blocks)
    def _(q):
        forward(q, 0)

    for c in swaps:
        c.wait()
    copies = []
    for d in list(range(1, groups)) + [0]:
        to = lax.rem(r + d, groups)

        @pl.loop(0, chunk)
        def _(u):
            forward(to * chunk + u, 1)

        if d:
            copies.append(copy(part.at[pl.ds(to * chunk, chunk)], land_a.at[d - 1], (to, s)))

    total = part[pl.ds(r * chunk, chunk)].astype(F32)
    for d, c in enumerate(copies):
        c.wait()
        total += land_a[d].astype(F32)
    for e in range(2):
        for i in range(pairs):
            pack_b[e, i] = total[:, e, i].astype(BF)
    cells = total[:, 0, 0]
    copies = []
    for k in range(1, slabs):
        e, i = k % 2, k // 2
        to = other_core(lax.rem(s + slabs - 2 * i, slabs), e)
        copies.append(copy(pack_b.at[e, i], land_b.at[k - 1], (r, to)))
    for k, c in enumerate(copies):
        c.wait()
        cells += land_b[k].astype(F32)
    resid = cells - value_ref[pl.ds(r * chunk, chunk)]
    score = resid / jnp.sqrt(1.0 + resid * resid / 4.0)
    score = jnp.where(seen_ref[pl.ds(r * chunk, chunk)] > 0.5, score, 0.0).astype(BF)
    mine_c[...] = score
    land_c[0, 0] = score
    copies = []
    for k in range(1, slabs):
        e, i = k % 2, k // 2
        to = other_core(lax.rem(s + 2 * i, slabs), e)
        copies.append(copy(mine_c, land_c.at[e, i], (r, to)))
    spread = [[] for _ in range(groups)]

    def hand_on(src, e, i):
        for d in range(1, groups):
            spread[d].append(copy(src, land_d.at[d - 1, e, i], (lax.rem(r + d, groups), s)))

    hand_on(mine_c, 0, 0)
    for k in range(1, slabs):
        e, i = k % 2, k // 2
        copies[k - 1].wait()
        hand_on(land_c.at[e, i], e, i)
    over = (((0,), (0,)), ((), ()))

    def backward(q, read):
        hm = jnp.concatenate([by_level(h_ref[q, e], code_ref[q, e] // 2, levels) for e in range(2)], 0)
        code = jnp.concatenate([code_ref[q, 0], code_ref[q, 1]], 0)
        straight = low_half((2 * n, TILE)) == (code % 2 == 0)
        score = jnp.concatenate([read(e, i) for e in range(2) for i in range(pairs)], 0).astype(F32)
        both = []
        for m in range(members):
            w = jnp.concatenate([pert_rows(q, 0, m), pert_rows(q, 1, m)], 0) * score
            both += [jnp.where(straight, w, 0.0).astype(BF), jnp.where(straight, 0.0, w).astype(BF)]
        out = lax.dot_general(hm, jnp.concatenate(both, 1), over, preferred_element_type=F32).astype(BF)
        for m in range(members):
            back_ref[q, m * depth : (m + 1) * depth, :] = out[:, 2 * TILE * m : 2 * TILE * (m + 1)]

    @pl.loop(0, chunk)
    def _(u):
        backward(r * chunk + u, lambda e, i: land_c[e, i, u])

    for d in range(1, groups):
        for c in spread[groups - d]:
            c.wait()
        source = lax.rem(r + d, groups)

        @pl.loop(0, chunk)
        def _(u):
            backward(source * chunk + u, lambda e, i: land_d[groups - 1 - d, e, i, u])


def gradient_kernel(back_ref, row_ref, col_ref, even_ref, odd_ref, out_ref):
    levels, rows, width = out_ref.shape[1:]
    half = width // 2
    over = (((1,), (1,)), ((), ()))
    chunk = 512
    blocks = back_ref.shape[0]
    ev = jnp.concatenate([back_ref[q, :, :TILE] for q in range(blocks)], 1)
    od = jnp.concatenate([back_ref[q, :, TILE:] for q in range(blocks)], 1)
    for c in range(0, half, chunk):
        e = lax.dot_general(ev, even_ref[c : c + chunk, :], over, preferred_element_type=F32)
        o = lax.dot_general(od, odd_ref[c : c + chunk, :], over, preferred_element_type=F32)
        for l in range(levels):
            el, ol = e[l * rows : (l + 1) * rows], o[l * rows : (l + 1) * rows]
            row = row_ref[l]
            out_ref[0, l, :, c : c + chunk] = (el + ol) * (row * col_ref[l : l + 1, c : c + chunk])
            out_ref[0, l, :, half + c : half + c + chunk] = (el - ol) * (
                row * col_ref[l : l + 1, half + c : half + c + chunk]
            )


def shards(control, perturbation, loc_row, loc_col, obs_tile, obs_count, obs_value):
    members, levels, rows, width = control.shape
    slabs = lax.axis_size("slab")
    groups = lax.axis_size("member")
    height = rows * slabs
    half = width // 2
    blocks = width // (2 * TILE)
    n_obs = obs_tile.shape[0]
    each = n_obs // blocks
    depth = levels * rows
    chunk = blocks // groups
    per_row = width // TILE
    mine = lax.axis_index("slab")
    assert slabs % blocks == 0 and blocks % groups == 0

    pairs = slabs // 2
    stack = members * each
    steps = n_obs // TILE
    cut = TILE // each
    flat_spec = pl.BlockSpec((steps, TILE), lambda g: (0, 0))
    cell_spec = pl.BlockSpec((TILE, TILE), lambda g: (g, 0))
    cell_shape = jax.ShapeDtypeStruct((n_obs, TILE), F32)
    picked, value, seen = pl.pallas_call(
        functools.partial(pick_kernel, rows, per_row, each),
        grid=(steps,),
        in_specs=[
            flat_spec,
            flat_spec,
            cell_spec,
            pl.BlockSpec((members, levels, rows, 2 * TILE * cut), lambda g: (0, 0, 0, g)),
        ],
        out_specs=[pl.BlockSpec((cut * stack, TILE), lambda g: (g, 0)), cell_spec, cell_spec],
        out_shape=[jax.ShapeDtypeStruct((blocks * stack, TILE), BF), cell_shape, cell_shape],
        name="pick",
    )(obs_tile.reshape(steps, TILE), obs_count.reshape(steps, TILE), obs_value, perturbation)
    picked, tile_in = lax.optimization_barrier((picked, obs_tile))
    tiles = pl.pallas_call(
        functools.partial(tiles_kernel, slabs),
        in_specs=[VM],
        out_specs=VM,
        out_shape=jax.ShapeDtypeStruct((2, pairs, n_obs // TILE, TILE), jnp.int32),
        scratch_shapes=[pltpu.SemaphoreType.DMA((slabs,)), pltpu.SemaphoreType.DMA((slabs,))],
        compiler_params=pltpu.CompilerParams(collective_id=1, has_side_effects=True),
        name="tiles",
    )(tile_in.reshape(-1, TILE))
    picked, tiles = lax.optimization_barrier((picked, tiles))
    value = value.reshape(blocks, each, TILE)
    seen = seen.reshape(blocks, each, TILE)
    pieces = [picked]
    for i in range(1, pairs):
        ring = [(k, (k + 2 * i) % slabs) for k in range(slabs)]
        pieces.append(lax.ppermute(picked, "slab", ring))

    column = jnp.arange(half, dtype=jnp.int32)
    swapped = column - column % TILE + (column % TILE + HALF) % TILE
    table_even = column_table(2 * column, width, half)
    table_odd = column_table(2 * swapped + 1, width, half)

    row_col = loc_row[:, :, None]
    table_spec = pl.BlockSpec((half, half), lambda m: (0, 0))
    row_spec = pl.BlockSpec((levels, rows, 1), lambda m: (0, 0, 0))
    col_spec = pl.BlockSpec((levels, width), lambda m: (0, 0))
    big_spec = pl.BlockSpec((1, levels, rows, width), lambda m: (m, 0, 0, 0))
    half_spec = pl.BlockSpec((blocks, depth, 2 * TILE), lambda m: (0, m, 0))
    half_shape = jax.ShapeDtypeStruct((blocks, members * depth, 2 * TILE), BF)
    flops = 4 * members * depth * half * half
    along = pl.pallas_call(
        along_kernel,
        grid=(members,),
        in_specs=[big_spec, row_spec, col_spec, table_spec, table_spec],
        out_specs=half_spec,
        out_shape=half_shape,
        cost_estimate=pl.CostEstimate(flops=flops, bytes_accessed=16 << 20, transcendentals=0),
        compiler_params=pltpu.CompilerParams(vmem_limit_bytes=56 << 20),
        name="along",
    )(control, row_col, loc_col, table_even, table_odd)

    e = jnp.arange(2, dtype=jnp.int32)[:, None]
    i = jnp.arange(pairs, dtype=jnp.int32)[None, :]
    source = (mine + e * (1 - 2 * (mine % 2)) - 2 * i) % slabs
    n = pairs * each
    listed = tiles.reshape(2, pairs, blocks, each)
    row_of = source[:, :, None, None] * rows + listed // per_row % rows
    code_of = listed // (rows * per_row) * 2 + listed % 2
    y = jnp.transpose(row_of, (2, 0, 1, 3)).reshape(blocks, 2, n, 1)
    code = jnp.transpose(code_of, (2, 0, 1, 3)).reshape(blocks, 2, n, 1)
    a = mine * rows + jnp.arange(rows, dtype=jnp.int32)
    angle = (2.0 * math.pi / height) * (y * a % height).astype(F32) - math.pi / 4
    table_h = (jnp.cos(angle) * math.sqrt(2.0 / height)).astype(BF)

    n_copies = pairs + 2 * (slabs - 1) + (groups - 1) * (slabs + 1)
    back = pl.pallas_call(
        functools.partial(core_kernel, members, levels, groups, slabs),
        in_specs=[VM] * (5 + pairs),
        out_specs=VM,
        out_shape=half_shape,
        scratch_shapes=[
            pltpu.VMEM((pairs, blocks * stack, TILE), BF),
            pltpu.VMEM((blocks, 2, pairs, each, TILE), BF),
            pltpu.VMEM((groups - 1, chunk, 2, pairs, each, TILE), BF),
            pltpu.VMEM((2, pairs, chunk, each, TILE), BF),
            pltpu.VMEM((slabs - 1, chunk, each, TILE), BF),
            pltpu.VMEM((chunk, each, TILE), BF),
            pltpu.VMEM((2, pairs, chunk, each, TILE), BF),
            pltpu.VMEM((groups - 1, 2, pairs, chunk, each, TILE), BF),
            pltpu.SemaphoreType.DMA((n_copies,)),
            pltpu.SemaphoreType.DMA((n_copies,)),
        ],
        compiler_params=pltpu.CompilerParams(collective_id=0, has_side_effects=True, vmem_limit_bytes=40 << 20),
        name="core",
    )(table_h, code, along, value, seen, *pieces)

    return pl.pallas_call(
        gradient_kernel,
        grid=(members,),
        in_specs=[half_spec, row_spec, col_spec, table_spec, table_spec],
        out_specs=big_spec,
        out_shape=jax.ShapeDtypeStruct(control.shape, F32),
        cost_estimate=pl.CostEstimate(flops=flops, bytes_accessed=16 << 20, transcendentals=0),
        compiler_params=pltpu.CompilerParams(vmem_limit_bytes=24 << 20),
        name="gradient",
    )(back, row_col, loc_col, table_even, table_odd)


def solution(mesh):
    placed = (
        P("member", None, "slab", None),
        P("member", None, "slab", None),
        P(None, "slab"),
        P(),
        P("slab"),
        P("slab"),
        P("slab", None),
    )
    return jax.shard_map(
        shards,
        mesh=mesh,
        in_specs=placed,
        out_specs=P("member", None, "slab", None),
        check_vma=False,
    )
```
